32 devices in a mesh: grp: 2 (over y), tile: 8 (over z, x), corner: 2 (over core).
Axes of the slice: x: 2, y: 2, z: 4, core: 2. Of those that a mesh axis runs over, the one named last changes fastest.
Arguments:
- mask_logits: float32 [768, 512], P(('grp', 'tile'), 'corner'), parts along dimension 0, may hold values from -1.5 to 1.5
- target: bfloat16 [768, 512], P(('grp', 'tile')), parts along dimension 0, may hold values from 0 to 1
- adam_first: float32 [768, 512], P(('grp', 'tile'), 'corner'), parts along dimension 0, may hold values from -1.5 to 1.5
- adam_second: float32 [768, 512], P(('grp', 'tile'), 'corner'), parts along dimension 0, may hold values from 0.05 to 0.2
- tile_counts: int32 [16, 4], P(('grp', 'tile')), parts along dimension 0, may hold values from 0 to 47
- kernels: float32 [2, 8, 2, 35, 35], P('corner'), may hold values from -0.15625 to 0.15625
- socs_weight: float32 [2, 8], P('corner'), may hold values from 0.03 to 0.3
- corner_dose: float32 [2], P('corner'), may hold values from 0.85 to 1.15
Outputs:
- out_logits: float32 [768, 512], P(('grp', 'tile'), 'corner'), parts along dimension 0
- out_first: float32 [768, 512], P(('grp', 'tile'), 'corner'), parts along dimension 0
- out_second: float32 [768, 512], P(('grp', 'tile'), 'corner'), parts along dimension 0
The draws below stay inside these ranges and needn't reach their ends.
There are 2 independent parts, one for each index of `grp`. The reference program is written for one: setup_inputs(seed, part) draws one part's arguments, and reference() takes and returns one part's arrays. A program takes and returns all parts, laid end to end along the dimension named above; an argument that names none is the same for every part. Nothing has to cross between parts.
All inputs are finite; a program needn't handle non-finite values.
Results may differ from the reference program's by a relative error of at most 0.013.
Values may be sent and summed in bfloat16 or wider, within the bound.
No kernel may reach another device: no remote copies, remote signals or barrier semaphores. Data moves between devices by JAX's collectives and lax.ppermute only.
A program may use at most 64 MiB of HBM per device.

```python
import math
import jax
import jax.numpy as jnp
from jax import lax

KERN = 8
KS = 35
TILE = 128
TPD = 4
BR = 48
ITERS = 2
HALF = 17
EXT = 82
LR = 88
BC = 512
LC = 640
STRIPS = 8
NR = 384
CORNERS = 2


def plant(result, rng, least, high):
    longest = result.shape.index(max(result.shape))
    spots = []
    for shift in (0, 1):
        where = [jax.random.randint(jax.random.fold_in(rng, axis), (), 0, length) for axis, length in enumerate(result.shape)]
        where[longest] = (where[longest] + shift) % result.shape[longest]
        spots.append(tuple(where))
    return result.at[spots[0]].set(least).at[spots[1]].set(high)


def block_levels(own_key, shape, cuts, low, high):
    def one(axis_at, shards_of):
        steps = jax.random.uniform(jax.random.fold_in(jax.random.fold_in(own_key, 6), axis_at), (shards_of,), jnp.float32, low / len(cuts), high / len(cuts))
        return jnp.repeat(jnp.exp(steps), shape[axis_at] // shards_of).reshape((-1,) + (1,) * (len(shape) - axis_at - 1))

    level = one(*cuts[0])
    for cut in cuts[1:]:
        level = level * one(*cut)
    return level


def centred(stream_key, dims, scale, most, shards=(), kind=jnp.bfloat16):
    drawn = scale * jax.random.normal(stream_key, dims, jnp.float32)
    if shards:
        drawn = drawn * block_levels(stream_key, dims, shards, -0.22, 0.18)
    return jnp.clip(drawn, -most, most).astype(kind)


def setup_inputs(seed: int = 0, part: int = 0) -> dict:
    seeds = jax.random.split(jax.random.key(seed), 9)
    own_keys = jax.random.split(jax.random.fold_in(seeds[8], part), 9)
    return {
        "mask_logits": jnp.clip(jax.random.uniform(own_keys[0], (NR, BC), jnp.float32, -1.5, 1.5) * block_levels(own_keys[0], (NR, BC), ((0, 8), (1, 2)), -0.4, 0.0), -1.5, 1.5),
        "target": jnp.clip(1.0 * jax.random.uniform(own_keys[1], (NR, BC), jnp.float32) ** block_levels(own_keys[1], (NR, BC), ((0, 8),), -0.2, 0.2), 0.0, 1.0).astype(jnp.bfloat16),
        "adam_first": jnp.clip(jax.random.uniform(own_keys[2], (NR, BC), jnp.float32, -1.5, 1.5) * block_levels(own_keys[2], (NR, BC), ((0, 8), (1, 2)), -0.4, 0.0), -1.5, 1.5),
        "adam_second": jnp.clip(jnp.exp(math.log(0.2) - 1.3862944 * jax.random.uniform(own_keys[3], (NR, BC), jnp.float32) ** block_levels(own_keys[3], (NR, BC), ((0, 8), (1, 2)), -0.2, 0.2)), 0.05, 0.2),
        "tile_counts": plant(jax.random.randint(own_keys[4], (STRIPS, TPD), 0, 48), jax.random.fold_in(own_keys[4], 1), 0, 47).astype(jnp.int32),
        "kernels": centred(seeds[5], (CORNERS, KERN, 2, KS, KS), (KS * KS) ** -0.5, 0.15625, ((0, 2),), jnp.float32),
        "socs_weight": jnp.clip(jnp.exp(math.log(0.3) - 2.3025852 * jax.random.uniform(seeds[6], (CORNERS, KERN), jnp.float32) ** block_levels(seeds[6], (CORNERS, KERN), ((0, 2),), -0.2, 0.2)), 0.03, 0.3),
        "corner_dose": jnp.clip(0.85 + 0.29999995 * jax.random.uniform(seeds[7], (CORNERS,), jnp.float32) ** block_levels(seeds[7], (CORNERS,), ((0, 2),), -0.2, 0.2), 0.85, 1.15),
    }


steep = 8.0
thresh = 0.5
loss_scale = 20.0
step_size = 0.05
beta_one = 0.9
beta_two = 0.999
adam_eps = 1e-08
prior_steps = 1000.0

def phase_table(first_index, second_index, length):
    wrapped = jnp.mod(first_index[:, None] * second_index[None, :], length)
    return wrapped.astype(jnp.float32) * (2.0 * math.pi / length)

def dft_tables(strip_rows, kernel_reach, width_all, rows_freq, cols_freq):
    ext_rows = strip_rows + 2 * kernel_reach
    angle_fwd_cols = phase_table(jnp.arange(width_all, dtype=jnp.int32), jnp.arange(cols_freq, dtype=jnp.int32), cols_freq)
    col_fwd = jnp.concatenate([jnp.cos(angle_fwd_cols), -jnp.sin(angle_fwd_cols)], axis=1).astype(jnp.bfloat16)
    angle_fwd_rows = phase_table(jnp.arange(rows_freq, dtype=jnp.int32), jnp.arange(ext_rows, dtype=jnp.int32), rows_freq)
    row_fwd = jnp.concatenate([jnp.cos(angle_fwd_rows), jnp.sin(angle_fwd_rows)], axis=1).astype(jnp.bfloat16)
    angle_inv_rows = phase_table(jnp.arange(strip_rows, dtype=jnp.int32) + kernel_reach, jnp.arange(rows_freq, dtype=jnp.int32), rows_freq)
    row_inv = jnp.concatenate([jnp.cos(angle_inv_rows), jnp.sin(angle_inv_rows)], axis=1).astype(jnp.bfloat16)
    angle_inv_cols = phase_table(jnp.arange(cols_freq, dtype=jnp.int32), jnp.arange(width_all, dtype=jnp.int32), cols_freq)
    cosine_inv = jnp.cos(angle_inv_cols)
    sine_inv = jnp.sin(angle_inv_cols)
    upper_block = jnp.concatenate([cosine_inv, sine_inv], axis=1)
    lower_block = jnp.concatenate([-sine_inv, cosine_inv], axis=1)
    col_inv = jnp.concatenate([upper_block, lower_block], axis=0).astype(jnp.bfloat16)
    return (col_fwd, row_fwd, row_inv, col_inv)

def kernel_spectra(kernels, kernel_reach, rows_freq, cols_freq):
    tap_count = kernels.shape[-1]
    offsets = jnp.arange(tap_count, dtype=jnp.int32) - kernel_reach
    angle_rows = phase_table(jnp.arange(rows_freq, dtype=jnp.int32), offsets, rows_freq)
    angle_cols = phase_table(jnp.arange(cols_freq, dtype=jnp.int32), offsets, cols_freq)
    cosine_rows = jnp.cos(angle_rows)
    sine_rows = jnp.sin(angle_rows)
    cosine_cols = jnp.cos(angle_cols)
    sine_cols = jnp.sin(angle_cols)
    real_taps = kernels[:, :, 0]
    imag_taps = kernels[:, :, 1]
    highest = lax.Precision.HIGHEST

    def contract(form, first_operand, second_operand):
        return jnp.einsum(form, first_operand, second_operand, precision=highest)
    half_real = contract('ckab,gb->ckag', real_taps, cosine_cols) + contract('ckab,gb->ckag', imag_taps, sine_cols)
    half_imag = contract('ckab,gb->ckag', imag_taps, cosine_cols) - contract('ckab,gb->ckag', real_taps, sine_cols)
    spec_real = contract('fa,ckag->ckfg', cosine_rows, half_real) + contract('fa,ckag->ckfg', sine_rows, half_imag)
    spec_imag = contract('fa,ckag->ckfg', cosine_rows, half_imag) - contract('fa,ckag->ckfg', sine_rows, half_real)
    return (spec_real, spec_imag)

def product(form, first_operand, second_operand):
    return jnp.einsum(form, first_operand.astype(jnp.float32), second_operand.astype(jnp.float32), precision=lax.Precision.HIGHEST)

def strip_gradient(mask_ext, target_strip, col_weight, spec_real, spec_imag, socs_weight, corner_dose, tables):
    col_fwd, row_fwd, row_inv, col_inv = tables
    ext_rows = mask_ext.shape[0]
    rows_freq = row_fwd.shape[0]
    cols_freq = col_fwd.shape[1] // 2
    strip_rows = row_inv.shape[0]
    width_all = col_fwd.shape[0]
    corner_count, kernel_count = socs_weight.shape
    normalize = 1.0 / (rows_freq * cols_freq)
    along_cols = jnp.dot(mask_ext, col_fwd, preferred_element_type=jnp.float32).astype(jnp.bfloat16)
    swapped = jnp.concatenate([along_cols[:, cols_freq:], -along_cols[:, :cols_freq]], axis=1)
    stacked = jnp.concatenate([along_cols, swapped], axis=0)
    spectrum = jnp.dot(row_fwd, stacked, preferred_element_type=jnp.float32)
    mask_real = spectrum[:, :cols_freq]
    mask_imag = spectrum[:, cols_freq:]
    prod_real = (mask_real * spec_real - mask_imag * spec_imag).astype(jnp.bfloat16)
    prod_imag = (mask_real * spec_imag + mask_imag * spec_real).astype(jnp.bfloat16)
    blocks = jnp.concatenate([jnp.concatenate([prod_real, prod_imag], axis=3), jnp.concatenate([-prod_imag, prod_real], axis=3)], axis=2)
    row_passed = product('jf,ckfg->ckjg', row_inv, blocks).astype(jnp.bfloat16)
    image_field = jnp.dot(row_passed.reshape(-1, 2 * cols_freq), col_inv, preferred_element_type=jnp.float32)
    image_field = image_field.reshape(corner_count, kernel_count, strip_rows, 2 * width_all) * normalize
    field_real = image_field[..., :width_all]
    field_imag = image_field[..., width_all:]
    weight_wide = socs_weight[:, :, None, None]
    intensity = lax.optimization_barrier(jnp.sum(weight_wide * (field_real * field_real + field_imag * field_imag), axis=1))
    dose_wide = corner_dose[:, None, None]
    resist = jax.nn.sigmoid(steep * (dose_wide * intensity - thresh))
    missed = resist - target_strip.astype(jnp.float32)[None]
    d_int = 2.0 * loss_scale * steep * col_weight[None, None, :] * missed * dose_wide * resist * (1.0 - resist)
    d_amplitude = 2.0 * weight_wide * d_int[:, None]
    d_field = jnp.concatenate([d_amplitude * field_real, d_amplitude * field_imag], axis=3).astype(jnp.bfloat16)
    d_inner = jnp.dot(d_field.reshape(-1, 2 * width_all), col_inv.T, preferred_element_type=jnp.float32) * normalize
    d_inner = d_inner.astype(jnp.bfloat16).reshape(corner_count, kernel_count, strip_rows, 2 * cols_freq)
    d_blocks = product('jf,ckjg->ckfg', row_inv, d_inner)
    upper_part = d_blocks[:, :, :rows_freq]
    lower_part = d_blocks[:, :, rows_freq:]
    d_prod_real = upper_part[..., :cols_freq] + lower_part[..., cols_freq:]
    d_prod_imag = upper_part[..., cols_freq:] - lower_part[..., :cols_freq]
    d_mask_real = lax.optimization_barrier(jnp.sum(d_prod_real * spec_real + d_prod_imag * spec_imag, axis=1))
    d_mask_imag = lax.optimization_barrier(jnp.sum(d_prod_imag * spec_real - d_prod_real * spec_imag, axis=1))
    d_spec = jnp.concatenate([d_mask_real, d_mask_imag], axis=2).astype(jnp.bfloat16)
    d_stacked = product('fj,cfg->cjg', row_fwd, d_spec)
    top_part = d_stacked[:, :ext_rows]
    bottom_part = d_stacked[:, ext_rows:]
    d_along = jnp.concatenate([top_part[..., :cols_freq] - bottom_part[..., cols_freq:], top_part[..., cols_freq:] + bottom_part[..., :cols_freq]], axis=2).astype(jnp.bfloat16)
    return product('cjg,hg->jh', d_along, col_fwd)

def reference(mask_logits, target, adam_first, adam_second, tile_counts, kernels, socs_weight, corner_dose):
    tables = dft_tables(BR, HALF, BC, LR, LC)
    spec_real, spec_imag = kernel_spectra(kernels, HALF, LR, LC)
    counts = tile_counts.astype(jnp.float32)
    col_weights = jnp.repeat(counts / (counts + 4.0), TILE, axis=1)
    target_strips = target.reshape(STRIPS, BR, BC)
    logits = mask_logits
    first = adam_first
    second = adam_second
    for iteration in range(ITERS):
        opacity = jax.nn.sigmoid(logits)
        mask_bf = opacity.astype(jnp.bfloat16)
        padded = jnp.pad(mask_bf, ((HALF, HALF), (0, 0)))

        def one_strip(pieces):
            strip_index, target_strip, col_weight = pieces
            start_row = strip_index * BR
            mask_ext = lax.dynamic_slice_in_dim(padded, start_row, EXT, 0)
            return strip_gradient(mask_ext, target_strip, col_weight, spec_real, spec_imag, socs_weight, corner_dose, tables)
        ext_grads = lax.map(one_strip, (jnp.arange(STRIPS, dtype=jnp.int32), target_strips, col_weights))
        upper_rims = ext_grads[:, :HALF]
        lower_rims = ext_grads[:, HALF + BR:]
        zero_rim = jnp.zeros((1, HALF, BC), jnp.float32)
        from_below = jnp.concatenate([upper_rims[1:], zero_rim], axis=0)
        from_above = jnp.concatenate([zero_rim, lower_rims[:-1]], axis=0)
        grad_mask = ext_grads[:, HALF:HALF + BR]
        grad_mask = grad_mask + jnp.pad(from_below, ((0, 0), (BR - HALF, 0), (0, 0)))
        grad_mask = grad_mask + jnp.pad(from_above, ((0, 0), (0, BR - HALF), (0, 0)))
        gradient = grad_mask.reshape(NR, BC) * opacity * (1.0 - opacity)
        count_now = prior_steps + iteration + 1.0
        first = beta_one * first + (1.0 - beta_one) * gradient
        second = beta_two * second + (1.0 - beta_two) * gradient * gradient
        first_hat = first / (1.0 - beta_one ** count_now)
        second_hat = second / (1.0 - beta_two ** count_now)
        logits = logits - step_size * first_hat / (jnp.sqrt(second_hat) + adam_eps)
    return (logits, first, second)
```

```python
import functools
import math

import jax
import jax.numpy as jnp
import numpy as np
from jax import lax
from jax.experimental import pallas as pl
from jax.experimental.pallas import tpu as pltpu
from jax.sharding import PartitionSpec as P

ITERS = 2

steep = 8.0
thresh = 0.5
loss_scale = 20.0
step_size = 0.05
beta_one = 0.9
beta_two = 0.999
adam_eps = 1e-08
prior_steps = 1000.0

LANES = 128
HALF_SPEC = 128
COL_LEN = 2 * HALF_SPEC

BF = jnp.bfloat16
F32 = jnp.float32


def up_to(value, unit):
    return -(-value // unit) * unit


class Plan:
    def __init__(self, strip_rows, width, taps):
        reach = taps // 2
        self.strip_rows, self.width, self.taps, self.reach = strip_rows, width, taps, reach
        self.field_rows = strip_rows + 2 * reach
        self.field_pad = up_to(self.field_rows, 8)
        self.ext_rows = strip_rows + 4 * reach
        self.row_len = up_to(self.ext_rows, 128)
        self.taps_pad = up_to(taps, 8)
        self.col_tiles = width // LANES - 1
        self.starts = [LANES * t for t in range(self.col_tiles)]
        assert width % LANES == 0 and self.col_tiles >= 2
        assert LANES > 4 * reach
        edge = LANES // 2 - 8
        self.bounds = [0] + [s + edge for s in self.starts[1:]] + [width]

        omega = 2.0 * math.pi * (np.arange(HALF_SPEC) + 0.5) / COL_LEN
        phi = 2.0 * math.pi * np.arange(self.row_len) / self.row_len
        rows = np.arange(self.row_len)

        fwd = []
        for t, start in enumerate(self.starts):
            x = start + np.arange(COL_LEN)
            keep = np.ones(COL_LEN)
            if t == 0:
                keep = keep * (x < COL_LEN - reach)
            if t == self.col_tiles - 1:
                keep = keep * (x >= start + reach)
            angle = (x - start)[:, None] * omega[None, :]
            fwd.append(np.concatenate([np.cos(angle), -np.sin(angle)], 1) * keep[:, None])
        self.col_fwd = np.stack(fwd)
        self.col_adj = self.col_fwd.transpose(0, 2, 1)

        scale = 2.0 / (COL_LEN * self.row_len)
        angle = omega[:, None] * np.arange(COL_LEN)[None, :]
        self.col_inv = np.concatenate([np.cos(angle), -np.sin(angle)], 0) * scale
        self.col_inv_adj = self.col_inv.T

        angle = phi[:, None] * rows[None, :]
        live = (rows < self.ext_rows)[None, :]
        c, s = np.cos(angle) * live, np.sin(angle) * live
        self.row_fwd = np.block([[c, s], [-s, c]])
        own = slice(2 * reach, 2 * reach + strip_rows)
        self.row_adj = np.block([[c[:, own].T, -s[:, own].T], [s[:, own].T, c[:, own].T]])

        angle = (np.arange(self.field_pad) + reach)[:, None] * phi[None, :]
        live = (np.arange(self.field_pad) < self.field_rows)[:, None]
        c, s = np.cos(angle) * live, np.sin(angle) * live
        self.row_inv = np.block([[c, -s], [s, c]])
        self.row_inv_adj = self.row_inv.T

        tap = np.arange(taps) - reach
        angle = tap[:, None] * omega[None, :]
        self.tap_cols = np.concatenate([np.cos(angle), -np.sin(angle)], 1)
        angle = phi[:, None] * tap[None, :]
        fill = ((0, 0), (0, self.taps_pad - taps))
        c, s = np.pad(np.cos(angle), fill), np.pad(np.sin(angle), fill)
        self.tap_rows = np.block([[c, s], [-s, c]])


@functools.lru_cache(maxsize=None)
def plan_of(strip_rows, width, taps):
    return Plan(strip_rows, width, taps)


def bf16_table(table):
    return np.asarray(table, np.float32).astype(BF)


def split_table(table):
    high = np.asarray(table, np.float32).astype(BF)
    low = (np.asarray(table, np.float64) - high.astype(np.float64)).astype(np.float32).astype(BF)
    return high, low


def dot(left, right):
    return lax.dot_general(left, right, (((1,), (0,)), ((), ())), preferred_element_type=F32)


def split(value):
    high = value.astype(BF)
    return high, (value - high.astype(F32)).astype(BF)


def spectra_body(plan, weight_ref, kern_ref, cols_hi_ref, cols_lo_ref, rows_ref, out_ref):
    count = kern_ref.shape[0]
    pad = plan.taps_pad - plan.taps
    for k in range(count):
        hi, lo = split(kern_ref[k])
        half = dot(hi, cols_hi_ref[...]) + dot(lo, cols_hi_ref[...]) + dot(hi, cols_lo_ref[...])
        half = jnp.concatenate([half, jnp.zeros((pad, half.shape[1]), F32)], axis=0)
        stacked = jnp.concatenate([half[:, :HALF_SPEC], half[:, HALF_SPEC:]], axis=0)
        hi, lo = split(stacked)
        spec = dot(rows_ref[...], jnp.concatenate([hi, hi, lo], axis=0))
        root = jnp.sqrt(jnp.full((8, LANES), weight_ref[k // 2], F32))[:1]
        out_ref[k] = spec * root


def kernel_spectra(plan, kernels, socs_weight):
    count = kernels.shape[1] * kernels.shape[2]
    taps = kernels.shape[-1]
    cols_hi, cols_lo = split_table(plan.tap_cols)
    rows_hi, rows_lo = split_table(plan.tap_rows)
    rows_all = np.concatenate([rows_hi, rows_lo, rows_hi], axis=1)
    vmem = pl.BlockSpec(memory_space=pltpu.VMEM)
    return pl.pallas_call(
        functools.partial(spectra_body, plan),
        out_shape=jax.ShapeDtypeStruct((count, 2 * plan.row_len, HALF_SPEC), F32),
        in_specs=[pl.BlockSpec(memory_space=pltpu.SMEM)] + [vmem] * 4,
        out_specs=vmem,
        name="spectra",
    )(
        socs_weight[0],
        kernels.reshape(count, taps, taps),
        jnp.asarray(cols_hi),
        jnp.asarray(cols_lo),
        jnp.asarray(rows_all),
    )


def gradient_body(
    plan,
    dose_ref,
    mask_ref,
    target_ref,
    weight_ref,
    spec_ref,
    col_fwd_ref,
    col_adj_ref,
    col_inv_ref,
    col_inv_adj_ref,
    row_fwd_ref,
    row_adj_ref,
    row_inv_ref,
    row_inv_adj_ref,
    out_ref,
    s_ref,
    field_ref,
    light_ref,
    acc_ref,
):
    tiles = plan.col_tiles
    rows = plan.row_len
    fr = plan.field_pad
    g = HALF_SPEC
    count = spec_ref.shape[0]

    along = []
    for t in range(tiles):
        window = mask_ref[:, plan.starts[t] : plan.starts[t] + COL_LEN]
        a = dot(window, col_fwd_ref[t])
        along.append(jnp.concatenate([a[:, :g], a[:, g:]], axis=0).astype(BF))
    s_ref[...] = dot(row_fwd_ref[...], jnp.concatenate(along, axis=1))
    light_ref[...] = jnp.zeros_like(light_ref)
    acc_ref[...] = jnp.zeros_like(acc_ref)

    def forward(pair, carry):
        for part in range(2):
            k = 2 * pair + part
            k_re, k_im = spec_ref[k, :rows], spec_ref[k, rows:]
            prods = []
            for t in range(tiles):
                lane = slice(t * g, t * g + g)
                s_re, s_im = s_ref[:rows, lane], s_ref[rows:, lane]
                p_re = (s_re * k_re - s_im * k_im).astype(BF)
                p_im = (s_re * k_im + s_im * k_re).astype(BF)
                prods.append(jnp.concatenate([p_re, p_im], axis=0))
            passed = dot(row_inv_ref[...], jnp.concatenate(prods, axis=1))
            for t in range(tiles):
                lane = slice(t * g, t * g + g)
                both = jnp.concatenate([passed[:fr, lane], passed[fr:, lane]], axis=1).astype(BF)
                field = dot(both, col_inv_ref[...])
                field_ref[k, t] = field
                light_ref[t] += field * field
        return carry

    lax.fori_loop(0, count // 2, forward, 0)

    dose = dose_ref[0]
    row = lax.broadcasted_iota(jnp.int32, (fr, COL_LEN), 0)
    col = lax.broadcasted_iota(jnp.int32, (fr, COL_LEN), 1)
    reach, strip = plan.reach, plan.strip_rows
    for t in range(tiles):
        lane = slice(plan.starts[t], plan.starts[t] + COL_LEN)
        resist = 1.0 / (1.0 + jnp.exp(-steep * (dose * light_ref[t] - thresh)))
        missed = resist - target_ref[:, lane].astype(F32)
        above, here, below = (weight_ref[i : i + 1, lane] for i in range(3))
        weight = jnp.where(row < reach, above, jnp.where(row < reach + strip, here, below))
        low, high = plan.bounds[t] - plan.starts[t], plan.bounds[t + 1] - plan.starts[t]
        kept = (row < plan.field_rows) & (col >= low) & (col < high)
        weight = jnp.where(kept, weight, 0.0)
        factor = 4.0 * loss_scale * steep * dose
        light_ref[t] = factor * weight * missed * resist * (1.0 - resist)

    def backward(pair, carry):
        for part in range(2):
            k = 2 * pair + part
            inner = []
            for t in range(tiles):
                d_field = (light_ref[t] * field_ref[k, t]).astype(BF)
                d = dot(d_field, col_inv_adj_ref[...])
                inner.append(jnp.concatenate([d[:, :g], d[:, g:]], axis=0).astype(BF))
            d_prod = dot(row_inv_adj_ref[...], jnp.concatenate(inner, axis=1))
            k_re, k_im = spec_ref[k, :rows], spec_ref[k, rows:]
            for t in range(tiles):
                lane = slice(t * g, t * g + g)
                d_re, d_im = d_prod[:rows, lane], d_prod[rows:, lane]
                acc_ref[:rows, lane] += d_re * k_re + d_im * k_im
                acc_ref[rows:, lane] += d_im * k_re - d_re * k_im
        return carry

    lax.fori_loop(0, count // 2, backward, 0)

    d_along = dot(row_adj_ref[...], acc_ref[...].astype(BF))
    parts = []
    for t in range(tiles):
        lane = slice(t * g, t * g + g)
        both = jnp.concatenate([d_along[:strip, lane], d_along[strip:, lane]], axis=1).astype(BF)
        parts.append(dot(both, col_adj_ref[t]))
    blocks = []
    for b in range(plan.width // LANES):
        terms = []
        for t in range(tiles):
            at = b * LANES - plan.starts[t]
            if 0 <= at < COL_LEN:
                terms.append(parts[t][:, at : at + LANES])
        blocks.append(functools.reduce(lambda x, y: x + y, terms))
    out_ref[...] = jnp.concatenate(blocks, axis=1)


def strip_gradient(plan, mask_ext, target_ext, weights, spec, corner_dose):
    tables = [
        jnp.asarray(bf16_table(table))
        for table in (
            plan.col_fwd,
            plan.col_adj,
            plan.col_inv,
            plan.col_inv_adj,
            plan.row_fwd,
            plan.row_adj,
            plan.row_inv,
            plan.row_inv_adj,
        )
    ]
    vmem = pl.BlockSpec(memory_space=pltpu.VMEM)
    count = spec.shape[0]
    spectrum = (2 * plan.row_len, plan.col_tiles * HALF_SPEC)
    image = (plan.col_tiles, plan.field_pad, COL_LEN)
    return pl.pallas_call(
        functools.partial(gradient_body, plan),
        out_shape=jax.ShapeDtypeStruct((plan.strip_rows, plan.width), F32),
        in_specs=[pl.BlockSpec(memory_space=pltpu.SMEM)] + [vmem] * (4 + len(tables)),
        out_specs=vmem,
        scratch_shapes=[
            pltpu.VMEM(spectrum, F32),
            pltpu.VMEM((count,) + image, F32),
            pltpu.VMEM(image, F32),
            pltpu.VMEM(spectrum, F32),
        ],
        name="gradient",
    )(corner_dose, mask_ext, target_ext, weights, spec, *tables)


def ring(value, axis, by):
    length = lax.axis_size(axis)
    return lax.ppermute(value, axis, [(i, (i + by) % length) for i in range(length)])


def other_corner(value):
    return lax.ppermute(value, "corner", [(0, 1), (1, 0)])


def neighbours(top, bottom):
    place = lax.axis_index("tile")
    last = lax.axis_size("tile") - 1
    above = ring(bottom, "tile", 1)
    below = ring(top, "tile", -1)
    zero = jnp.zeros((), top.dtype)
    return jnp.where(place == 0, zero, above), jnp.where(place == last, zero, below)


def per_device(
    mask_logits, target, adam_first, adam_second, tile_counts, kernels, socs_weight, corner_dose
):
    strip_rows, half_width = mask_logits.shape
    width = target.shape[1]
    plan = plan_of(strip_rows, width, kernels.shape[-1])
    reach = plan.reach
    halo = 2 * reach
    corner = lax.axis_index("corner")

    def whole(own, other):
        left = jnp.where(corner == 0, own, other)
        right = jnp.where(corner == 0, other, own)
        return jnp.concatenate([left, right], axis=-1)

    def own_half(value):
        return jnp.where(corner == 0, value[..., :half_width], value[..., half_width:])

    state = jnp.stack([mask_logits, adam_first, adam_second])
    state = whole(state, other_corner(state))
    logits, first, second = state[0], state[1], state[2]
    opacity = jax.nn.sigmoid(logits)
    mask_bf = opacity.astype(BF)
    counts = jnp.repeat(tile_counts.astype(F32), width // tile_counts.shape[1], axis=1)

    counts_bf = counts.astype(BF)
    above, below = neighbours(
        jnp.concatenate([mask_bf[:halo], target[:reach], counts_bf], axis=0),
        jnp.concatenate([mask_bf[-halo:], target[-reach:], counts_bf], axis=0),
    )
    spec = kernel_spectra(plan, kernels, socs_weight)

    def extended(above_rows, own, below_rows, total):
        have = above_rows.shape[0] + own.shape[0] + below_rows.shape[0]
        blank = jnp.zeros((total - have, own.shape[1]), own.dtype)
        return jnp.concatenate([above_rows, own, below_rows, blank], axis=0)

    target_ext = extended(
        above[halo : halo + reach], target, below[halo : halo + reach], plan.field_pad
    )
    near = jnp.concatenate([above[halo + reach :].astype(F32), counts, below[halo + reach :].astype(F32)])
    near = jnp.pad(near, ((0, 5), (0, 0)))
    weights = near / (near + 4.0)
    above, below = above[:halo], below[:halo]

    for iteration in range(ITERS):
        if iteration:
            opacity = jax.nn.sigmoid(logits)
            mask_bf = opacity.astype(BF)
            above, below = neighbours(mask_bf[:halo], mask_bf[-halo:])
        mask_ext = extended(above, mask_bf, below, plan.row_len)
        partial = strip_gradient(plan, mask_ext, target_ext, weights, spec, corner_dose)
        if iteration < ITERS - 1:
            summed = partial + other_corner(partial.astype(BF)).astype(F32)
        else:
            mine = own_half(partial)
            theirs = jnp.where(corner == 0, partial[:, half_width:], partial[:, :half_width])
            summed = mine + other_corner(theirs.astype(BF)).astype(F32)
            opacity, logits = own_half(opacity), own_half(logits)
            first, second = own_half(first), own_half(second)
        gradient = summed * opacity * (1.0 - opacity)
        count_now = prior_steps + iteration + 1.0
        first = beta_one * first + (1.0 - beta_one) * gradient
        second = beta_two * second + (1.0 - beta_two) * gradient * gradient
        first_hat = first / (1.0 - beta_one**count_now)
        second_hat = second / (1.0 - beta_two**count_now)
        logits = logits - step_size * first_hat / (jnp.sqrt(second_hat) + adam_eps)
    return (logits, first, second)


def solution(mesh):
    return jax.shard_map(
        per_device,
        mesh=mesh,
        in_specs=(
            P(("grp", "tile"), "corner"),
            P(("grp", "tile"), None),
            P(("grp", "tile"), "corner"),
            P(("grp", "tile"), "corner"),
            P(("grp", "tile"), None),
            P("corner", None, None, None, None),
            P("corner", None),
            P("corner"),
        ),
        out_specs=(
            P(("grp", "tile"), "corner"),
            P(("grp", "tile"), "corner"),
            P(("grp", "tile"), "corner"),
        ),
        check_vma=False,
    )
```

```python
import functools
import math

import jax
import jax.numpy as jnp
import numpy as np
from jax import lax
from jax.experimental import pallas as pl
from jax.experimental.pallas import tpu as pltpu
from jax.sharding import PartitionSpec as P

ITERS = 2

steep = 8.0
thresh = 0.5
loss_scale = 20.0
step_size = 0.05
beta_one = 0.9
beta_two = 0.999
adam_eps = 1e-08
prior_steps = 1000.0

LANES = 128
HALF_SPEC = 128
COL_LEN = 2 * HALF_SPEC
CHUNK = 16
GROUP = 2

BF = jnp.bfloat16
F32 = jnp.float32


def up_to(value, unit):
    return -(-value // unit) * unit


class Plan:
    def __init__(self, strip_rows, width, taps):
        reach = taps // 2
        self.strip_rows, self.width, self.taps, self.reach = strip_rows, width, taps, reach
        self.field_rows = strip_rows + 2 * reach
        self.field_pad = up_to(self.field_rows, 8)
        self.ext_rows = strip_rows + 4 * reach
        self.row_len = up_to(self.ext_rows, 128)
        self.taps_pad = up_to(taps, 8)
        self.col_tiles = width // LANES - 1
        self.starts = [LANES * t for t in range(self.col_tiles)]
        assert width % LANES == 0 and self.col_tiles >= 2
        assert LANES > 4 * reach
        edge = LANES // 2 - 8
        self.bounds = [0] + [s + edge for s in self.starts[1:]] + [width]

        omega = 2.0 * math.pi * (np.arange(HALF_SPEC) + 0.5) / COL_LEN
        phi = 2.0 * math.pi * np.arange(self.row_len) / self.row_len
        rows = np.arange(self.row_len)

        fwd = []
        for t, start in enumerate(self.starts):
            x = start + np.arange(COL_LEN)
            keep = np.ones(COL_LEN)
            if t == 0:
                keep = keep * (x < COL_LEN - reach)
            if t == self.col_tiles - 1:
                keep = keep * (x >= start + reach)
            angle = (x - start)[:, None] * omega[None, :]
            fwd.append(np.concatenate([np.cos(angle), -np.sin(angle)], 1) * keep[:, None])
        self.col_fwd = np.stack(fwd)
        self.col_adj = self.col_fwd.transpose(0, 2, 1)

        scale = 2.0 / (COL_LEN * self.row_len)
        angle = omega[:, None] * np.arange(COL_LEN)[None, :]
        self.col_inv = np.concatenate([np.cos(angle), -np.sin(angle)], 0) * scale
        self.col_inv_adj = self.col_inv.T

        angle = phi[:, None] * rows[None, :]
        live = (rows < self.ext_rows)[None, :]
        c, s = np.cos(angle) * live, np.sin(angle) * live
        mixed = np.arange(2 * self.row_len).reshape(2, -1, CHUNK).transpose(1, 0, 2).reshape(-1)
        self.row_fwd = np.block([[c, s], [-s, c]])[mixed]
        own = slice(2 * reach, 2 * reach + strip_rows)
        self.row_adj = np.block([[c[:, own].T, -s[:, own].T], [s[:, own].T, c[:, own].T]])[:, mixed]

        angle = (np.arange(self.field_pad) + reach)[:, None] * phi[None, :]
        live = (np.arange(self.field_pad) < self.field_rows)[:, None]
        c, s = np.cos(angle) * live, np.sin(angle) * live
        self.row_inv = np.block([[c, -s], [s, c]])[:, mixed]
        self.row_inv_adj = self.row_inv.T

        tap = np.arange(taps) - reach
        angle = tap[:, None] * omega[None, :]
        self.tap_cols = np.concatenate([np.cos(angle), -np.sin(angle)], 1)
        angle = phi[:, None] * tap[None, :]
        fill = ((0, 0), (0, self.taps_pad - taps))
        c, s = np.pad(np.cos(angle), fill), np.pad(np.sin(angle), fill)
        self.tap_rows = np.block([[c, s], [-s, c]])[mixed]


@functools.lru_cache(maxsize=None)
def plan_of(strip_rows, width, taps):
    return Plan(strip_rows, width, taps)


def bf16_table(table):
    return np.asarray(table, np.float32).astype(BF)


def split_table(table):
    high = np.asarray(table, np.float32).astype(BF)
    low = (np.asarray(table, np.float64) - high.astype(np.float64)).astype(np.float32).astype(BF)
    return high, low


def dot(left, right):
    return lax.dot_general(left, right, (((1,), (0,)), ((), ())), preferred_element_type=F32)


def split(value):
    high = value.astype(BF)
    return high, (value - high.astype(F32)).astype(BF)


def spectra_body(plan, weight_ref, kern_ref, cols_hi_ref, cols_lo_ref, rows_ref, out_ref):
    count = kern_ref.shape[0]
    pad = plan.taps_pad - plan.taps
    for k in range(count):
        hi, lo = split(kern_ref[k])
        half = dot(hi, cols_hi_ref[...]) + dot(lo, cols_hi_ref[...]) + dot(hi, cols_lo_ref[...])
        half = jnp.concatenate([half, jnp.zeros((pad, half.shape[1]), F32)], axis=0)
        stacked = jnp.concatenate([half[:, :HALF_SPEC], half[:, HALF_SPEC:]], axis=0)
        hi, lo = split(stacked)
        spec = dot(rows_ref[...], jnp.concatenate([hi, hi, lo], axis=0))
        root = jnp.sqrt(jnp.full((8, LANES), weight_ref[k // 2], F32))[:1]
        out_ref[k] = spec * root


def kernel_spectra(plan, kernels, socs_weight):
    count = kernels.shape[1] * kernels.shape[2]
    taps = kernels.shape[-1]
    cols_hi, cols_lo = split_table(plan.tap_cols)
    rows_hi, rows_lo = split_table(plan.tap_rows)
    rows_all = np.concatenate([rows_hi, rows_lo, rows_hi], axis=1)
    vmem = pl.BlockSpec(memory_space=pltpu.VMEM)
    return pl.pallas_call(
        functools.partial(spectra_body, plan),
        out_shape=jax.ShapeDtypeStruct((count, 2 * plan.row_len, HALF_SPEC), F32),
        in_specs=[pl.BlockSpec(memory_space=pltpu.SMEM)] + [vmem] * 4,
        out_specs=vmem,
        compiler_params=pltpu.CompilerParams(vmem_limit_bytes=16 * 1024 * 1024),
        name="spectra",
    )(
        socs_weight[0],
        kernels.reshape(count, taps, taps),
        jnp.asarray(cols_hi),
        jnp.asarray(cols_lo),
        jnp.asarray(rows_all),
    )


def gradient_body(
    plan,
    dose_ref,
    mask_ref,
    target_ref,
    weight_ref,
    spec_ref,
    col_fwd_ref,
    col_adj_ref,
    col_inv_ref,
    col_inv_adj_ref,
    row_fwd_ref,
    row_adj_ref,
    row_inv_ref,
    row_inv_adj_ref,
    out_ref,
    s_ref,
    field_ref,
    light_ref,
    acc_ref,
    hold_ref,
    back_ref,
):
    tiles = plan.col_tiles
    rows = plan.row_len
    fr = plan.field_pad
    g = HALF_SPEC
    count = spec_ref.shape[0]

    along = []
    for t in range(tiles):
        window = mask_ref[:, plan.starts[t] : plan.starts[t] + COL_LEN]
        a = dot(window, col_fwd_ref[t])
        along.append(jnp.concatenate([a[:, :g], a[:, g:]], axis=0).astype(BF))
    s_ref[...] = dot(row_fwd_ref[...], jnp.concatenate(along, axis=1))
    light_ref[...] = jnp.zeros_like(light_ref)
    acc_ref[...] = jnp.zeros_like(acc_ref)
    chunks = [(at, at + CHUNK, at + 2 * CHUNK) for at in range(0, 2 * rows, 2 * CHUNK)]

    groups = count // GROUP

    def multiply(group):
        passed = []
        for t in range(tiles):
            lane = slice(t * g, t * g + g)
            prods = [[] for _ in range(GROUP)]
            for a, b, c in chunks:
                s_re, s_im = s_ref[a:b, lane], s_ref[b:c, lane]
                for part in range(GROUP):
                    k = GROUP * group + part
                    k_re, k_im = spec_ref[k, a:b], spec_ref[k, b:c]
                    prods[part].append((s_re * k_re - s_im * k_im).astype(BF))
                    prods[part].append((s_re * k_im + s_im * k_re).astype(BF))
            block = jnp.concatenate([jnp.concatenate(p, axis=0) for p in prods], axis=1)
            passed.append(dot(row_inv_ref[...], block))
        stack = []
        for t in range(tiles):
            for part in range(GROUP):
                lane = slice(part * g, part * g + g)
                stack.append(jnp.concatenate([passed[t][:fr, lane], passed[t][fr:, lane]], axis=1))
        hold_ref[group % 2] = jnp.concatenate(stack, axis=0).astype(BF)

    def image(group):
        field = dot(hold_ref[group % 2], col_inv_ref[...])
        field_ref[group] = field
        for t in range(tiles):
            total = light_ref[t]
            for part in range(GROUP):
                at = (GROUP * t + part) * fr
                one = field[at : at + fr]
                total = total + one * one
            light_ref[t] = total

    def forward(group, carry):
        image(group)
        multiply(group + 1)
        return carry

    multiply(0)
    lax.fori_loop(0, groups - 1, forward, 0)
    image(groups - 1)

    dose = dose_ref[0]
    row = lax.broadcasted_iota(jnp.int32, (fr, COL_LEN), 0)
    col = lax.broadcasted_iota(jnp.int32, (fr, COL_LEN), 1)
    reach, strip = plan.reach, plan.strip_rows
    for t in range(tiles):
        lane = slice(plan.starts[t], plan.starts[t] + COL_LEN)
        resist = 1.0 / (1.0 + jnp.exp(-steep * (dose * light_ref[t] - thresh)))
        missed = resist - target_ref[:, lane].astype(F32)
        above, here, below = (weight_ref[i : i + 1, lane] for i in range(3))
        weight = jnp.where(row < reach, above, jnp.where(row < reach + strip, here, below))
        low, high = plan.bounds[t] - plan.starts[t], plan.bounds[t + 1] - plan.starts[t]
        kept = (row < plan.field_rows) & (col >= low) & (col < high)
        weight = jnp.where(kept, weight, 0.0)
        factor = 4.0 * loss_scale * steep * dose
        light_ref[t] = factor * weight * missed * resist * (1.0 - resist)

    def image_back(group):
        stack = []
        for t in range(tiles):
            for part in range(GROUP):
                at = (GROUP * t + part) * fr
                stack.append(light_ref[t] * field_ref[group, at : at + fr])
        inner = dot(jnp.concatenate(stack, axis=0).astype(BF), col_inv_adj_ref[...])
        for t in range(tiles):
            block = []
            for part in range(GROUP):
                at = (GROUP * t + part) * fr
                d = inner[at : at + fr]
                block.append(jnp.concatenate([d[:, :g], d[:, g:]], axis=0))
            back_ref[group % 2, t] = jnp.concatenate(block, axis=1).astype(BF)

    def multiply_back(group):
        for t in range(tiles):
            lane = slice(t * g, t * g + g)
            d_prod = dot(row_inv_adj_ref[...], back_ref[group % 2, t])
            for a, b, c in chunks:
                sum_re, sum_im = acc_ref[a:b, lane], acc_ref[b:c, lane]
                for part in range(GROUP):
                    k = GROUP * group + part
                    k_re, k_im = spec_ref[k, a:b], spec_ref[k, b:c]
                    at = slice(part * g, part * g + g)
                    d_re, d_im = d_prod[a:b, at], d_prod[b:c, at]
                    sum_re = sum_re + (d_re * k_re + d_im * k_im)
                    sum_im = sum_im + (d_im * k_re - d_re * k_im)
                acc_ref[a:b, lane] = sum_re
                acc_ref[b:c, lane] = sum_im

    def backward(group, carry):
        multiply_back(group)
        image_back(group + 1)
        return carry

    image_back(0)
    lax.fori_loop(0, groups - 1, backward, 0)
    multiply_back(groups - 1)

    d_along = dot(row_adj_ref[...], acc_ref[...].astype(BF))
    parts = []
    for t in range(tiles):
        lane = slice(t * g, t * g + g)
        both = jnp.concatenate([d_along[:strip, lane], d_along[strip:, lane]], axis=1).astype(BF)
        parts.append(dot(both, col_adj_ref[t]))
    blocks = []
    for b in range(plan.width // LANES):
        terms = []
        for t in range(tiles):
            at = b * LANES - plan.starts[t]
            if 0 <= at < COL_LEN:
                terms.append(parts[t][:, at : at + LANES])
        blocks.append(functools.reduce(lambda x, y: x + y, terms))
    out_ref[...] = jnp.concatenate(blocks, axis=1)


def strip_gradient(plan, mask_ext, target_ext, weights, spec, corner_dose):
    tables = [
        jnp.asarray(bf16_table(table))
        for table in (
            plan.col_fwd,
            plan.col_adj,
            plan.col_inv,
            plan.col_inv_adj,
            plan.row_fwd,
            plan.row_adj,
            plan.row_inv,
            plan.row_inv_adj,
        )
    ]
    vmem = pl.BlockSpec(memory_space=pltpu.VMEM)
    count = spec.shape[0]
    spectrum = (2 * plan.row_len, plan.col_tiles * HALF_SPEC)
    image = (plan.col_tiles, plan.field_pad, COL_LEN)
    return pl.pallas_call(
        functools.partial(gradient_body, plan),
        out_shape=jax.ShapeDtypeStruct((plan.strip_rows, plan.width), F32),
        in_specs=[pl.BlockSpec(memory_space=pltpu.SMEM)] + [vmem] * (4 + len(tables)),
        out_specs=vmem,
        scratch_shapes=[
            pltpu.VMEM(spectrum, F32),
            pltpu.VMEM((count // GROUP, GROUP * plan.col_tiles * plan.field_pad, COL_LEN), F32),
            pltpu.VMEM(image, F32),
            pltpu.VMEM(spectrum, F32),
            pltpu.VMEM((2, GROUP * plan.col_tiles * plan.field_pad, COL_LEN), BF),
            pltpu.VMEM((2, plan.col_tiles, 2 * plan.field_pad, GROUP * HALF_SPEC), BF),
        ],
        compiler_params=pltpu.CompilerParams(vmem_limit_bytes=32 * 1024 * 1024),
        name="gradient",
    )(corner_dose, mask_ext, target_ext, weights, spec, *tables)


def ring(value, axis, by):
    length = lax.axis_size(axis)
    return lax.ppermute(value, axis, [(i, (i + by) % length) for i in range(length)])


def other_corner(value):
    return lax.ppermute(value, "corner", [(0, 1), (1, 0)])


def neighbours(top, bottom):
    place = lax.axis_index("tile")
    last = lax.axis_size("tile") - 1
    above = ring(bottom, "tile", 1)
    below = ring(top, "tile", -1)
    zero = jnp.zeros((), top.dtype)
    return jnp.where(place == 0, zero, above), jnp.where(place == last, zero, below)


def per_device(
    mask_logits, target, adam_first, adam_second, tile_counts, kernels, socs_weight, corner_dose
):
    strip_rows, half_width = mask_logits.shape
    width = target.shape[1]
    plan = plan_of(strip_rows, width, kernels.shape[-1])
    reach = plan.reach
    halo = 2 * reach
    corner = lax.axis_index("corner")

    def whole(own, other):
        left = jnp.where(corner == 0, own, other)
        right = jnp.where(corner == 0, other, own)
        return jnp.concatenate([left, right], axis=-1)

    def own_half(value):
        return jnp.where(corner == 0, value[..., :half_width], value[..., half_width:])

    state = jnp.stack([mask_logits, adam_first, adam_second])
    state = whole(state, other_corner(state))
    logits, first, second = state[0], state[1], state[2]
    opacity = jax.nn.sigmoid(logits)
    mask_bf = opacity.astype(BF)
    counts = jnp.repeat(tile_counts.astype(F32), width // tile_counts.shape[1], axis=1)

    counts_bf = counts.astype(BF)
    above, below = neighbours(
        jnp.concatenate([mask_bf[:halo], target[:reach], counts_bf], axis=0),
        jnp.concatenate([mask_bf[-halo:], target[-reach:], counts_bf], axis=0),
    )
    spec = kernel_spectra(plan, kernels, socs_weight)

    def extended(above_rows, own, below_rows, total):
        have = above_rows.shape[0] + own.shape[0] + below_rows.shape[0]
        blank = jnp.zeros((total - have, own.shape[1]), own.dtype)
        return jnp.concatenate([above_rows, own, below_rows, blank], axis=0)

    target_ext = extended(
        above[halo : halo + reach], target, below[halo : halo + reach], plan.field_pad
    )
    near = jnp.concatenate([above[halo + reach :].astype(F32), counts, below[halo + reach :].astype(F32)])
    near = jnp.pad(near, ((0, 5), (0, 0)))
    weights = near / (near + 4.0)
    above, below = above[:halo], below[:halo]

    for iteration in range(ITERS):
        if iteration:
            opacity = jax.nn.sigmoid(logits)
            mask_bf = opacity.astype(BF)
            above, below = neighbours(mask_bf[:halo], mask_bf[-halo:])
        mask_ext = extended(above, mask_bf, below, plan.row_len)
        partial = strip_gradient(plan, mask_ext, target_ext, weights, spec, corner_dose)
        if iteration < ITERS - 1:
            summed = partial + other_corner(partial.astype(BF)).astype(F32)
        else:
            mine = own_half(partial)
            theirs = jnp.where(corner == 0, partial[:, half_width:], partial[:, :half_width])
            summed = mine + other_corner(theirs.astype(BF)).astype(F32)
            opacity, logits = own_half(opacity), own_half(logits)
            first, second = own_half(first), own_half(second)
        gradient = summed * opacity * (1.0 - opacity)
        count_now = prior_steps + iteration + 1.0
        first = beta_one * first + (1.0 - beta_one) * gradient
        second = beta_two * second + (1.0 - beta_two) * gradient * gradient
        first_hat = first / (1.0 - beta_one**count_now)
        second_hat = second / (1.0 - beta_two**count_now)
        logits = logits - step_size * first_hat / (jnp.sqrt(second_hat) + adam_eps)
    return (logits, first, second)


def solution(mesh):
    return jax.shard_map(
        per_device,
        mesh=mesh,
        in_specs=(
            P(("grp", "tile"), "corner"),
            P(("grp", "tile"), None),
            P(("grp", "tile"), "corner"),
            P(("grp", "tile"), "corner"),
            P(("grp", "tile"), None),
            P("corner", None, None, None, None),
            P("corner", None),
            P("corner"),
        ),
        out_specs=(
            P(("grp", "tile"), "corner"),
            P(("grp", "tile"), "corner"),
            P(("grp", "tile"), "corner"),
        ),
        check_vma=False,
    )
```

```python
import functools
import math

import jax
import jax.numpy as jnp
import numpy as np
from jax import lax
from jax.experimental import pallas as pl
from jax.experimental.pallas import tpu as pltpu
from jax.sharding import PartitionSpec as P


ITERS = 2

steep = 8.0
thresh = 0.5
loss_scale = 20.0
step_size = 0.05
beta_one = 0.9
beta_two = 0.999
adam_eps = 1e-08
prior_steps = 1000.0

LANES = 128
HALF_SPEC = 128
MIDDLE = 0.5
COL_LEN = 2 * HALF_SPEC
CHUNK = 16
GROUP = 2

BF = jnp.bfloat16
F32 = jnp.float32


def up_to(value, unit):
    return -(-value // unit) * unit


class Plan:
    def __init__(self, strip_rows, width, taps):
        reach = taps // 2
        self.strip_rows, self.width, self.taps, self.reach = strip_rows, width, taps, reach
        self.field_rows = strip_rows + 2 * reach
        self.field_pad = up_to(self.field_rows, 8)
        self.ext_rows = strip_rows + 4 * reach
        self.row_len = up_to(self.ext_rows, 128)
        self.taps_pad = up_to(taps, 8)
        self.col_tiles = width // LANES - 1
        self.starts = [LANES * t for t in range(self.col_tiles)]
        assert width % LANES == 0 and self.col_tiles >= 2
        assert LANES > 4 * reach
        edge = LANES // 2 - 8
        self.bounds = [0] + [s + edge for s in self.starts[1:]] + [width]

        omega = 2.0 * math.pi * (np.arange(HALF_SPEC) + 0.5) / COL_LEN
        phi = 2.0 * math.pi * np.arange(self.row_len) / self.row_len
        rows = np.arange(self.row_len)

        fwd = []
        for t, start in enumerate(self.starts):
            x = start + np.arange(COL_LEN)
            keep = np.ones(COL_LEN)
            if t == 0:
                keep = keep * (x < COL_LEN - reach)
            if t == self.col_tiles - 1:
                keep = keep * (x >= start + reach)
            angle = (x - start)[:, None] * omega[None, :]
            fwd.append(np.concatenate([np.cos(angle), -np.sin(angle)], 1) * keep[:, None])
        self.col_fwd = np.stack(fwd)
        edges = []
        for x in (np.arange(-reach, 0), COL_LEN + np.arange(reach)):
            angle = x[:, None] * omega[None, :]
            edge = -MIDDLE * np.concatenate([np.cos(angle), -np.sin(angle)], 1).sum(0)
            edges += split_table(edge)
        self.edges = np.stack(edges)
        self.col_adj = self.col_fwd.transpose(0, 2, 1)

        scale = 2.0 / (COL_LEN * self.row_len)
        angle = omega[:, None] * np.arange(COL_LEN)[None, :]
        self.col_inv = np.concatenate([np.cos(angle), -np.sin(angle)], 0) * scale
        self.col_inv_adj = self.col_inv.T

        angle = phi[:, None] * rows[None, :]
        live = (rows < self.ext_rows)[None, :]
        c, s = np.cos(angle) * live, np.sin(angle) * live
        mixed = np.arange(2 * self.row_len).reshape(2, -1, CHUNK).transpose(1, 0, 2).reshape(-1)
        self.row_fwd = np.block([[c, s], [-s, c]])[mixed]
        own = slice(2 * reach, 2 * reach + strip_rows)
        self.row_adj = np.block([[c[:, own].T, -s[:, own].T], [s[:, own].T, c[:, own].T]])[:, mixed]

        angle = (np.arange(self.field_pad) + reach)[:, None] * phi[None, :]
        live = (np.arange(self.field_pad) < self.field_rows)[:, None]
        c, s = np.cos(angle) * live, np.sin(angle) * live
        self.row_inv = np.block([[c, -s], [s, c]])[:, mixed]
        self.row_inv_adj = self.row_inv.T

        tap = np.arange(taps) - reach
        angle = tap[:, None] * omega[None, :]
        self.tap_cols = np.concatenate([np.cos(angle), -np.sin(angle)], 1)
        angle = phi[:, None] * tap[None, :]
        fill = ((0, 0), (0, self.taps_pad - taps))
        c, s = np.pad(np.cos(angle), fill), np.pad(np.sin(angle), fill)
        self.tap_rows = np.block([[c, s], [-s, c]])[mixed]


        rows_hi, rows_lo = split_table(self.tap_rows)
        cols_hi, cols_lo = split_table(self.tap_cols)
        parts = {
            "col_fwd": self.col_fwd.reshape(-1, COL_LEN),
            "col_adj": self.col_adj.reshape(-1, COL_LEN),
            "col_inv": self.col_inv,
            "col_inv_adj": self.col_inv_adj,
            "row_fwd": self.row_fwd,
            "row_adj": self.row_adj,
            "row_inv": self.row_inv,
            "row_inv_adj": self.row_inv_adj,
            "edges": self.edges,
        }
        tap_parts = {
            "tap_rows": np.concatenate([rows_hi, rows_lo, rows_hi], axis=1),
            "tap_hi": cols_hi,
            "tap_lo": cols_lo,
        }
        self.where = {}
        self.packed = self.pack(parts)
        self.tap_packed = self.pack(tap_parts)

    def pack(self, parts):
        packed, at = [], 0
        wide = max(part.shape[1] for part in parts.values())
        for name, part in parts.items():
            part = np.asarray(part, np.float32).astype(BF)
            self.where[name] = (at, part.shape[0], part.shape[1])
            fill = up_to(part.shape[0], CHUNK) - part.shape[0]
            packed.append(np.pad(part, ((0, fill), (0, wide - part.shape[1]))))
            at += part.shape[0] + fill
        return np.concatenate(packed, axis=0)

    def table(self, ref, name, block=None):
        at, rows, cols = self.where[name]
        if block is not None:
            at, rows = at + block * COL_LEN, COL_LEN
        return ref[at : at + rows, :cols]


@functools.lru_cache(maxsize=None)
def plan_of(strip_rows, width, taps):
    return Plan(strip_rows, width, taps)


def split_table(table):
    high = np.asarray(table, np.float32).astype(BF)
    low = (np.asarray(table, np.float64) - high.astype(np.float64)).astype(np.float32).astype(BF)
    return high, low


def dot(left, right):
    return lax.dot_general(left, right, (((1,), (0,)), ((), ())), preferred_element_type=F32)


def split(value):
    high = value.astype(BF)
    return high, (value - high.astype(F32)).astype(BF)


def fetch_body(
    logits_hbm,
    first_hbm,
    second_hbm,
    target_hbm,
    counts_hbm,
    mask_ref,
    state_ref,
    target_ref,
    counts_ref,
    flags_ref,
    counts_smem,
    sems,
):
    pairs = (
        (logits_hbm, state_ref.at[0]),
        (counts_hbm, counts_smem),
        (target_hbm, target_ref),
        (first_hbm, state_ref.at[1]),
        (second_hbm, state_ref.at[2]),
    )
    copies = [pltpu.make_async_copy(a, b, sems.at[i]) for i, (a, b) in enumerate(pairs)]
    for copy in copies:
        copy.start()
    place, corner = lax.axis_index("tile"), lax.axis_index("corner")
    facts = (corner == 0, place == 0, place == lax.axis_size("tile") - 1)
    for i, fact in enumerate(facts):
        flags_ref[i] = jnp.full((8, LANES), jnp.where(fact, 1.0, 0.0), F32)
    copies[0].wait()
    mask = (1.0 / (1.0 + jnp.exp(-state_ref[0]))).astype(BF)
    mask_ref[...] = (mask.astype(F32) - MIDDLE).astype(BF)
    for copy in copies[1:]:
        copy.wait()
    tiles = counts_smem.shape[1]
    wide = counts_ref.shape[1] // tiles
    for tile in range(tiles):
        value = counts_smem[0, tile].astype(F32)
        counts_ref[:, tile * wide : (tile + 1) * wide] = jnp.full((8, wide), value, F32)


def fetch(mask_logits, adam_first, adam_second, target, tile_counts):
    args = (mask_logits, adam_first, adam_second, target, tile_counts)
    shape = mask_logits.shape
    outs = (
        jax.ShapeDtypeStruct(shape, BF),
        jax.ShapeDtypeStruct((3,) + shape, F32),
        jax.ShapeDtypeStruct(target.shape, BF),
        jax.ShapeDtypeStruct((8, target.shape[1]), F32),
        jax.ShapeDtypeStruct((3, 8, LANES), F32),
    )
    return pl.pallas_call(
        fetch_body,
        out_shape=outs,
        in_specs=[pl.BlockSpec(memory_space=pltpu.HBM)] * len(args),
        out_specs=tuple(pl.BlockSpec(memory_space=pltpu.VMEM) for _ in outs),
        scratch_shapes=[
            pltpu.SMEM(tile_counts.shape, jnp.int32),
            pltpu.SemaphoreType.DMA((len(args),)),
        ],
        compiler_params=pltpu.CompilerParams(vmem_limit_bytes=4 * 1024 * 1024),
        name="fetch",
    )(*(pltpu.with_memory_space_constraint(value, pltpu.HBM) for value in args))


def spectra_body(
    plan,
    weight_hbm,
    kern_hbm,
    table_hbm,
    out_ref,
    level_ref,
    weight_ref,
    kern_ref,
    table_ref,
    sems,
):
    copies = [
        pltpu.make_async_copy(kern_hbm, kern_ref, sems.at[0]),
        pltpu.make_async_copy(table_hbm, table_ref, sems.at[1]),
        pltpu.make_async_copy(weight_hbm, weight_ref, sems.at[2]),
    ]
    for copy in copies:
        copy.start()
    for copy in copies:
        copy.wait()
    count = out_ref.shape[0]
    pad = plan.taps_pad - plan.taps
    stack, sums = [], []
    for k in range(count):
        taps = kern_ref[k // 2, :, k % 2, :]
        sums.append(jnp.sum(taps, axis=0, keepdims=True))
        stack.append(jnp.concatenate([taps, jnp.zeros((pad, plan.taps), F32)], axis=0))
    hi, lo = split(jnp.concatenate(stack, axis=0))
    sums = MIDDLE * jnp.sum(jnp.concatenate(sums, axis=0), axis=1, keepdims=True)
    sums = jnp.broadcast_to(sums, (count, COL_LEN))
    cols_hi, cols_lo = plan.table(table_ref, "tap_hi"), plan.table(table_ref, "tap_lo")
    half = dot(hi, cols_hi) + dot(lo, cols_hi) + dot(hi, cols_lo)
    for k in range(0, count, 2):
        both = []
        for part in (k, k + 1):
            one = half[part * plan.taps_pad : (part + 1) * plan.taps_pad]
            both.append(jnp.concatenate([one[:, :HALF_SPEC], one[:, HALF_SPEC:]], axis=0))
        hi, lo = split(jnp.concatenate(both, axis=1))
        spec = dot(plan.table(table_ref, "tap_rows"), jnp.concatenate([hi, hi, lo], axis=0))
        root_wide = jnp.sqrt(jnp.full((8, COL_LEN), weight_ref[0, k // 2], F32))
        root = root_wide[:1, :HALF_SPEC]
        for part in (k, k + 1):
            level_ref[part] = root_wide * sums[part : part + 1]
        out_ref[k] = spec[:, :HALF_SPEC] * root
        out_ref[k + 1] = spec[:, HALF_SPEC:] * root


def kernel_spectra(plan, kernels, socs_weight):
    count = kernels.shape[1] * kernels.shape[2]
    taps = kernels[0].transpose(0, 2, 1, 3)
    tables = plan.tap_packed
    hbm = pl.BlockSpec(memory_space=pltpu.HBM)
    return pl.pallas_call(
        functools.partial(spectra_body, plan),
        out_shape=(
            jax.ShapeDtypeStruct((count, 2 * plan.row_len, HALF_SPEC), F32),
            jax.ShapeDtypeStruct((count, 8, COL_LEN), F32),
        ),
        in_specs=[hbm] * 3,
        out_specs=(pl.BlockSpec(memory_space=pltpu.VMEM), pl.BlockSpec(memory_space=pltpu.VMEM)),
        scratch_shapes=[
            pltpu.SMEM(socs_weight.shape, F32),
            pltpu.VMEM(taps.shape, F32),
            pltpu.VMEM(tables.shape, BF),
            pltpu.SemaphoreType.DMA((3,)),
        ],
        compiler_params=pltpu.CompilerParams(vmem_limit_bytes=4 * 1024 * 1024),
        name="spectra",
    )(
        *(
            pltpu.with_memory_space_constraint(value, pltpu.HBM)
            for value in (socs_weight, taps, jnp.asarray(tables))
        ),
    )


def gradient_body(
    plan,
    dose_ref,
    mask_ref,
    target_ref,
    weight_ref,
    spec_ref,
    level_ref,
    table_ref,
    out_ref,
    s_ref,
    field_ref,
    light_ref,
    acc_ref,
    hold_ref,
    back_ref,
):
    tiles = plan.col_tiles
    rows = plan.row_len
    fr = plan.field_pad
    g = HALF_SPEC
    count = spec_ref.shape[0]

    along = []
    edges = plan.table(table_ref, "edges").astype(F32)
    for t in range(tiles):
        window = mask_ref[:, plan.starts[t] : plan.starts[t] + COL_LEN]
        a = dot(window, plan.table(table_ref, "col_fwd", t))
        if t == 0:
            a = a + (edges[0:1] + edges[1:2])
        if t == tiles - 1:
            a = a + (edges[2:3] + edges[3:4])
        along.append(jnp.concatenate([a[:, :g], a[:, g:]], axis=0).astype(BF))
    s_ref[...] = dot(plan.table(table_ref, "row_fwd"), jnp.concatenate(along, axis=1))
    light_ref[...] = jnp.zeros_like(light_ref)
    acc_ref[...] = jnp.zeros_like(acc_ref)
    chunks = [(at, at + CHUNK, at + 2 * CHUNK) for at in range(0, 2 * rows, 2 * CHUNK)]

    groups = count // GROUP

    def multiply(group):
        passed = []
        for t in range(tiles):
            lane = slice(t * g, t * g + g)
            prods = [[] for _ in range(GROUP)]
            for a, b, c in chunks:
                s_re, s_im = s_ref[a:b, lane], s_ref[b:c, lane]
                for part in range(GROUP):
                    k = GROUP * group + part
                    k_re, k_im = spec_ref[k, a:b], spec_ref[k, b:c]
                    prods[part].append((s_re * k_re - s_im * k_im).astype(BF))
                    prods[part].append((s_re * k_im + s_im * k_re).astype(BF))
            block = jnp.concatenate([jnp.concatenate(p, axis=0) for p in prods], axis=1)
            passed.append(dot(plan.table(table_ref, "row_inv"), block))
        stack = []
        for t in range(tiles):
            for part in range(GROUP):
                lane = slice(part * g, part * g + g)
                stack.append(jnp.concatenate([passed[t][:fr, lane], passed[t][fr:, lane]], axis=1))
        hold_ref[group % 2] = jnp.concatenate(stack, axis=0).astype(BF)

    def image(group):
        field = dot(hold_ref[group % 2], plan.table(table_ref, "col_inv"))
        for t in range(tiles):
            total = light_ref[t]
            for part in range(GROUP):
                at = (GROUP * t + part) * fr
                one = field[at : at + fr] + level_ref[GROUP * group + part, :1]
                field_ref[group, at : at + fr] = one
                total = total + one * one
            light_ref[t] = total

    def forward(group, carry):
        image(group)
        multiply(group + 1)
        return carry

    multiply(0)
    lax.fori_loop(0, groups - 1, forward, 0)
    image(groups - 1)

    dose = dose_ref[:1, :1]
    row = lax.broadcasted_iota(jnp.int32, (fr, COL_LEN), 0)
    col = lax.broadcasted_iota(jnp.int32, (fr, COL_LEN), 1)
    reach, strip = plan.reach, plan.strip_rows
    for t in range(tiles):
        lane = slice(plan.starts[t], plan.starts[t] + COL_LEN)
        resist = 1.0 / (1.0 + jnp.exp(-steep * (dose * light_ref[t] - thresh)))
        missed = resist - target_ref[:, lane].astype(F32)
        above, here, below = (weight_ref[i : i + 1, lane] for i in range(3))
        weight = jnp.where(row < reach, above, jnp.where(row < reach + strip, here, below))
        low, high = plan.bounds[t] - plan.starts[t], plan.bounds[t + 1] - plan.starts[t]
        kept = (row < plan.field_rows) & (col >= low) & (col < high)
        weight = jnp.where(kept, weight, 0.0)
        factor = 4.0 * loss_scale * steep * dose
        light_ref[t] = factor * weight * missed * resist * (1.0 - resist)

    def image_back(group):
        stack = []
        for t in range(tiles):
            for part in range(GROUP):
                at = (GROUP * t + part) * fr
                stack.append(light_ref[t] * field_ref[group, at : at + fr])
        inner = dot(jnp.concatenate(stack, axis=0).astype(BF), plan.table(table_ref, "col_inv_adj"))
        for t in range(tiles):
            block = []
            for part in range(GROUP):
                at = (GROUP * t + part) * fr
                d = inner[at : at + fr]
                block.append(jnp.concatenate([d[:, :g], d[:, g:]], axis=0))
            back_ref[group % 2, t] = jnp.concatenate(block, axis=1).astype(BF)

    def multiply_back(group):
        for t in range(tiles):
            lane = slice(t * g, t * g + g)
            d_prod = dot(plan.table(table_ref, "row_inv_adj"), back_ref[group % 2, t])
            for a, b, c in chunks:
                sum_re, sum_im = acc_ref[a:b, lane], acc_ref[b:c, lane]
                for part in range(GROUP):
                    k = GROUP * group + part
                    k_re, k_im = spec_ref[k, a:b], spec_ref[k, b:c]
                    at = slice(part * g, part * g + g)
                    d_re, d_im = d_prod[a:b, at], d_prod[b:c, at]
                    sum_re = sum_re + (d_re * k_re + d_im * k_im)
                    sum_im = sum_im + (d_im * k_re - d_re * k_im)
                acc_ref[a:b, lane] = sum_re
                acc_ref[b:c, lane] = sum_im

    def backward(group, carry):
        multiply_back(group)
        image_back(group + 1)
        return carry

    image_back(0)
    lax.fori_loop(0, groups - 1, backward, 0)
    multiply_back(groups - 1)

    d_along = dot(plan.table(table_ref, "row_adj"), acc_ref[...].astype(BF))
    parts = []
    for t in range(tiles):
        lane = slice(t * g, t * g + g)
        both = jnp.concatenate([d_along[:strip, lane], d_along[strip:, lane]], axis=1).astype(BF)
        parts.append(dot(both, plan.table(table_ref, "col_adj", t)))
    blocks = []
    for b in range(plan.width // LANES):
        terms = []
        for t in range(tiles):
            at = b * LANES - plan.starts[t]
            if 0 <= at < COL_LEN:
                terms.append(parts[t][:, at : at + LANES])
        blocks.append(functools.reduce(lambda x, y: x + y, terms))
    out_ref[...] = jnp.concatenate(blocks, axis=1)


def strip_gradient(plan, mask_ext, target_ext, weights, spec, dose, tables):
    vmem = pl.BlockSpec(memory_space=pltpu.VMEM)
    count = spec[0].shape[0]
    spectrum = (2 * plan.row_len, plan.col_tiles * HALF_SPEC)
    image = (plan.col_tiles, plan.field_pad, COL_LEN)
    return pl.pallas_call(
        functools.partial(gradient_body, plan),
        out_shape=jax.ShapeDtypeStruct((plan.strip_rows, plan.width), F32),
        in_specs=[vmem] * 7,
        out_specs=vmem,
        scratch_shapes=[
            pltpu.VMEM(spectrum, F32),
            pltpu.VMEM((count // GROUP, GROUP * plan.col_tiles * plan.field_pad, COL_LEN), F32),
            pltpu.VMEM(image, F32),
            pltpu.VMEM(spectrum, F32),
            pltpu.VMEM((2, GROUP * plan.col_tiles * plan.field_pad, COL_LEN), BF),
            pltpu.VMEM((2, plan.col_tiles, 2 * plan.field_pad, GROUP * HALF_SPEC), BF),
        ],
        compiler_params=pltpu.CompilerParams(vmem_limit_bytes=12 * 1024 * 1024),
        name="gradient",
    )(dose, mask_ext, target_ext, weights, *spec, tables)


def other_corner(value):
    return lax.ppermute(value, "corner", [(0, 1), (1, 0)])


def neighbours(flags, top, bottom, blank):
    strips = lax.axis_size("tile")
    first_corner, highest, lowest = flags
    cycle = [(2 * i, 2 * i + 2) for i in range(strips - 1)] + [(2 * strips - 2, 2 * strips - 1)]
    cycle += [(2 * i + 1, 2 * i - 1) for i in range(1, strips)] + [(1, 0)]
    message = jnp.where(first_corner, bottom, top)
    got = lax.ppermute(message, ("tile", "corner"), cycle)
    shared = other_corner(got)
    above = jnp.where(highest, blank, jnp.where(first_corner, got, shared))
    below = jnp.where(lowest, blank, jnp.where(first_corner, shared, got))
    return above, below


def per_device(
    mask_logits, target, adam_first, adam_second, tile_counts, kernels, socs_weight, corner_dose
):
    strip_rows, half_width = mask_logits.shape
    width = target.shape[1]
    plan = plan_of(strip_rows, width, kernels.shape[-1])
    reach = plan.reach
    halo = 2 * reach

    def whole(own, other):
        left = jnp.where(first_corner, own, other)
        right = jnp.where(first_corner, other, own)
        return jnp.concatenate([left, right], axis=-1)

    def own_half(value):
        return jnp.where(first_corner, value[..., :half_width], value[..., half_width:])

    def extended(above_rows, own, below_rows, total):
        have = above_rows.shape[0] + own.shape[0] + below_rows.shape[0]
        blank = jnp.zeros((total - have, own.shape[1]), own.dtype)
        return jnp.concatenate([above_rows, own, below_rows, blank], axis=0)

    tables = jnp.asarray(plan.packed)

    mask_half, state, target, counts, facts = fetch(
        mask_logits, adam_first, adam_second, target, tile_counts
    )
    flags = [facts[i, :1, :1] > 0.5 for i in range(3)]
    first_corner = flags[0]
    dose = jnp.broadcast_to(corner_dose[None], (8, LANES))
    counts = counts[:1]
    counts_bf = counts.astype(BF)
    other_half = other_corner(mask_half)
    mask_bf = whole(mask_half, other_half)
    above, below = neighbours(
        flags,
        jnp.concatenate([mask_bf[:halo], target[:reach], counts_bf], axis=0),
        jnp.concatenate([mask_bf[-halo:], target[-reach:], counts_bf], axis=0),
        jnp.where(jnp.arange(halo + reach + 1)[:, None] < halo, -MIDDLE, 0.0).astype(BF),
    )
    spec = kernel_spectra(plan, kernels, socs_weight)
    target_ext = extended(
        above[halo : halo + reach], target, below[halo : halo + reach], plan.field_pad
    )
    near = jnp.concatenate(
        [above[halo + reach :].astype(F32), counts, below[halo + reach :].astype(F32)]
    )
    near = jnp.pad(near, ((0, 5), (0, 0)))
    weights = near / (near + 4.0)
    above, below = above[:halo], below[:halo]
    mask_ext = extended(above, mask_bf, below, plan.row_len)
    state = whole(state, other_corner(state))
    partial = strip_gradient(plan, mask_ext, target_ext, weights, spec, dose, tables)

    logits, first, second = state[0], state[1], state[2]
    opacity = jax.nn.sigmoid(logits)
    for iteration in range(ITERS):
        if iteration:
            opacity = jax.nn.sigmoid(logits)
            mask_bf = (lax.reduce_precision(opacity, 8, 7) - MIDDLE).astype(BF)
            blank = jnp.full((halo, 1), -MIDDLE, BF)
            above, below = neighbours(flags, mask_bf[:halo], mask_bf[-halo:], blank)
            mask_ext = extended(above, mask_bf, below, plan.row_len)
            partial = strip_gradient(plan, mask_ext, target_ext, weights, spec, dose, tables)
        if iteration < ITERS - 1:
            summed = partial + other_corner(partial.astype(BF)).astype(F32)
        else:
            mine = own_half(partial)
            theirs = jnp.where(first_corner, partial[:, half_width:], partial[:, :half_width])
            summed = mine + other_corner(theirs.astype(BF)).astype(F32)
            opacity, logits = own_half(opacity), own_half(logits)
            first, second = own_half(first), own_half(second)
        gradient = summed * opacity * (1.0 - opacity)
        count_now = prior_steps + iteration + 1.0
        first = beta_one * first + (1.0 - beta_one) * gradient
        second = beta_two * second + (1.0 - beta_two) * gradient * gradient
        first_hat = first / (1.0 - beta_one**count_now)
        second_hat = second / (1.0 - beta_two**count_now)
        logits = logits - step_size * first_hat / (jnp.sqrt(second_hat) + adam_eps)
    return (logits, first, second)


def solution(mesh):
    return jax.shard_map(
        per_device,
        mesh=mesh,
        in_specs=(
            P(("grp", "tile"), "corner"),
            P(("grp", "tile"), None),
            P(("grp", "tile"), "corner"),
            P(("grp", "tile"), "corner"),
            P(("grp", "tile"), None),
            P("corner", None, None, None, None),
            P("corner", None),
            P("corner"),
        ),
        out_specs=(
            P(("grp", "tile"), "corner"),
            P(("grp", "tile"), "corner"),
            P(("grp", "tile"), "corner"),
        ),
        check_vma=False,
    )
```

```python
import functools
import math

import jax
import jax.numpy as jnp
import numpy as np
from jax import lax
from jax.experimental import pallas as pl
from jax.experimental.pallas import tpu as pltpu
from jax.sharding import PartitionSpec as P


ITERS = 2

steep = 8.0
thresh = 0.5
loss_scale = 20.0
step_size = 0.05
beta_one = 0.9
beta_two = 0.999
adam_eps = 1e-08
prior_steps = 1000.0

LANES = 128
HALF_SPEC = 128
MIDDLE = 0.5
COL_LEN = 2 * HALF_SPEC
CHUNK = 16
GROUP = 2

BF = jnp.bfloat16
F32 = jnp.float32


def up_to(value, unit):
    return -(-value // unit) * unit


class Plan:
    def __init__(self, strip_rows, width, taps):
        reach = taps // 2
        self.strip_rows, self.width, self.taps, self.reach = strip_rows, width, taps, reach
        self.field_rows = strip_rows + 2 * reach
        self.field_pad = up_to(self.field_rows, 8)
        self.ext_rows = strip_rows + 4 * reach
        self.row_len = up_to(self.ext_rows, 128)
        self.taps_pad = up_to(taps, 8)
        self.col_tiles = width // LANES - 1
        self.starts = [LANES * t for t in range(self.col_tiles)]
        assert width % LANES == 0 and self.col_tiles >= 2
        assert LANES > 4 * reach
        edge = LANES // 2 - 8
        self.bounds = [0] + [s + edge for s in self.starts[1:]] + [width]

        omega = 2.0 * math.pi * (np.arange(HALF_SPEC) + 0.5) / COL_LEN
        phi = 2.0 * math.pi * np.arange(self.row_len) / self.row_len
        rows = np.arange(self.row_len)

        fwd = []
        for t, start in enumerate(self.starts):
            x = start + np.arange(COL_LEN)
            keep = np.ones(COL_LEN)
            if t == 0:
                keep = keep * (x < COL_LEN - reach)
            if t == self.col_tiles - 1:
                keep = keep * (x >= start + reach)
            angle = (x - start)[:, None] * omega[None, :]
            fwd.append(np.concatenate([np.cos(angle), -np.sin(angle)], 1) * keep[:, None])
        self.col_fwd = np.stack(fwd)
        edges = []
        for x in (np.arange(-reach, 0), COL_LEN + np.arange(reach)):
            angle = x[:, None] * omega[None, :]
            edge = -MIDDLE * np.concatenate([np.cos(angle), -np.sin(angle)], 1).sum(0)
            edges += split_table(edge)
        self.edges = np.stack(edges)
        self.col_adj = self.col_fwd.transpose(0, 2, 1)

        scale = 2.0 / (COL_LEN * self.row_len)
        angle = omega[:, None] * np.arange(COL_LEN)[None, :]
        self.col_inv = np.concatenate([np.cos(angle), -np.sin(angle)], 0) * scale
        self.col_inv_adj = self.col_inv.T

        angle = phi[:, None] * rows[None, :]
        live = (rows < self.ext_rows)[None, :]
        c, s = np.cos(angle) * live, np.sin(angle) * live
        mixed = np.arange(2 * self.row_len).reshape(2, -1, CHUNK).transpose(1, 0, 2).reshape(-1)
        self.row_fwd = np.block([[c, s], [-s, c]])[mixed]
        own = slice(2 * reach, 2 * reach + strip_rows)
        self.row_adj = np.block([[c[:, own].T, -s[:, own].T], [s[:, own].T, c[:, own].T]])[:, mixed]

        angle = (np.arange(self.field_pad) + reach)[:, None] * phi[None, :]
        live = (np.arange(self.field_pad) < self.field_rows)[:, None]
        c, s = np.cos(angle) * live, np.sin(angle) * live
        self.row_inv = np.block([[c, -s], [s, c]])[:, mixed]
        self.row_inv_adj = self.row_inv.T

        tap = np.arange(taps) - reach
        angle = tap[:, None] * omega[None, :]
        self.tap_cols = np.concatenate([np.cos(angle), -np.sin(angle)], 1)
        angle = phi[:, None] * tap[None, :]
        fill = ((0, 0), (0, self.taps_pad - taps))
        c, s = np.pad(np.cos(angle), fill), np.pad(np.sin(angle), fill)
        self.tap_rows = np.block([[c, s], [-s, c]])[mixed]


        rows_hi, rows_lo = split_table(self.tap_rows)
        cols_hi, cols_lo = split_table(self.tap_cols)
        parts = {
            "col_fwd": self.col_fwd.reshape(-1, COL_LEN),
            "col_adj": self.col_adj.reshape(-1, COL_LEN),
            "col_inv": self.col_inv,
            "col_inv_adj": self.col_inv_adj,
            "row_fwd": self.row_fwd,
            "row_adj": self.row_adj,
            "row_inv": self.row_inv,
            "row_inv_adj": self.row_inv_adj,
            "edges": self.edges,
        }
        tap_parts = {
            "tap_rows": np.concatenate([rows_hi, rows_lo, rows_hi], axis=1),
            "tap_hi": cols_hi,
            "tap_lo": cols_lo,
        }
        self.where = {}
        self.packed = self.pack(parts)
        self.tap_packed = self.pack(tap_parts)

    def pack(self, parts):
        packed, at = [], 0
        wide = max(part.shape[1] for part in parts.values())
        for name, part in parts.items():
            part = np.asarray(part, np.float32).astype(BF)
            self.where[name] = (at, part.shape[0], part.shape[1])
            fill = up_to(part.shape[0], CHUNK) - part.shape[0]
            packed.append(np.pad(part, ((0, fill), (0, wide - part.shape[1]))))
            at += part.shape[0] + fill
        return np.concatenate(packed, axis=0)

    def table(self, ref, name, block=None):
        at, rows, cols = self.where[name]
        if block is not None:
            at, rows = at + block * COL_LEN, COL_LEN
        return ref[at : at + rows, :cols]


@functools.lru_cache(maxsize=None)
def plan_of(strip_rows, width, taps):
    return Plan(strip_rows, width, taps)


def split_table(table):
    high = np.asarray(table, np.float32).astype(BF)
    low = (np.asarray(table, np.float64) - high.astype(np.float64)).astype(np.float32).astype(BF)
    return high, low


def dot(left, right):
    return lax.dot_general(left, right, (((1,), (0,)), ((), ())), preferred_element_type=F32)


def split(value):
    high = value.astype(BF)
    return high, (value - high.astype(F32)).astype(BF)


def fetch_body(
    logits_hbm,
    first_hbm,
    second_hbm,
    target_hbm,
    counts_hbm,
    mask_ref,
    state_ref,
    target_ref,
    counts_ref,
    flags_ref,
    counts_smem,
    sems,
):
    pairs = (
        (logits_hbm, state_ref.at[0]),
        (counts_hbm, counts_smem),
        (target_hbm, target_ref),
        (first_hbm, state_ref.at[1]),
        (second_hbm, state_ref.at[2]),
    )
    copies = [pltpu.make_async_copy(a, b, sems.at[i]) for i, (a, b) in enumerate(pairs)]
    for copy in copies:
        copy.start()
    place, corner = lax.axis_index("tile"), lax.axis_index("corner")
    facts = (corner == 0, place == 0, place == lax.axis_size("tile") - 1)
    for i, fact in enumerate(facts):
        flags_ref[i] = jnp.full((8, LANES), jnp.where(fact, 1.0, 0.0), F32)
    copies[0].wait()
    mask = (1.0 / (1.0 + jnp.exp(-state_ref[0]))).astype(BF)
    mask_ref[...] = (mask.astype(F32) - MIDDLE).astype(BF)
    for copy in copies[1:]:
        copy.wait()
    tiles = counts_smem.shape[1]
    wide = counts_ref.shape[1] // tiles
    for tile in range(tiles):
        value = counts_smem[0, tile].astype(F32)
        counts_ref[:, tile * wide : (tile + 1) * wide] = jnp.full((8, wide), value, F32)


def fetch(mask_logits, adam_first, adam_second, target, tile_counts):
    args = (mask_logits, adam_first, adam_second, target, tile_counts)
    shape = mask_logits.shape
    outs = (
        jax.ShapeDtypeStruct(shape, BF),
        jax.ShapeDtypeStruct((3,) + shape, F32),
        jax.ShapeDtypeStruct(target.shape, BF),
        jax.ShapeDtypeStruct((8, target.shape[1]), F32),
        jax.ShapeDtypeStruct((3, 8, LANES), F32),
    )
    return pl.pallas_call(
        fetch_body,
        out_shape=outs,
        in_specs=[pl.BlockSpec(memory_space=pltpu.HBM)] * len(args),
        out_specs=tuple(pl.BlockSpec(memory_space=pltpu.VMEM) for _ in outs),
        scratch_shapes=[
            pltpu.SMEM(tile_counts.shape, jnp.int32),
            pltpu.SemaphoreType.DMA((len(args),)),
        ],
        compiler_params=pltpu.CompilerParams(vmem_limit_bytes=4 * 1024 * 1024),
        name="fetch",
    )(*(pltpu.with_memory_space_constraint(value, pltpu.HBM) for value in args))


def spectra_body(
    plan,
    weight_hbm,
    kern_hbm,
    table_hbm,
    out_ref,
    level_ref,
    weight_ref,
    kern_ref,
    table_ref,
    sems,
):
    copies = [
        pltpu.make_async_copy(kern_hbm, kern_ref, sems.at[0]),
        pltpu.make_async_copy(table_hbm, table_ref, sems.at[1]),
        pltpu.make_async_copy(weight_hbm, weight_ref, sems.at[2]),
    ]
    for copy in copies:
        copy.start()
    for copy in copies:
        copy.wait()
    count = out_ref.shape[0]
    pad = plan.taps_pad - plan.taps
    stack, sums = [], []
    for k in range(count):
        taps = kern_ref[k // 2, :, k % 2, :]
        sums.append(jnp.sum(taps, axis=0, keepdims=True))
        stack.append(jnp.concatenate([taps, jnp.zeros((pad, plan.taps), F32)], axis=0))
    hi, lo = split(jnp.concatenate(stack, axis=0))
    sums = MIDDLE * jnp.sum(jnp.concatenate(sums, axis=0), axis=1, keepdims=True)
    sums = jnp.broadcast_to(sums, (count, COL_LEN))
    cols_hi, cols_lo = plan.table(table_ref, "tap_hi"), plan.table(table_ref, "tap_lo")
    half = dot(hi, cols_hi) + dot(lo, cols_hi) + dot(hi, cols_lo)
    for k in range(0, count, 2):
        both = []
        for part in (k, k + 1):
            one = half[part * plan.taps_pad : (part + 1) * plan.taps_pad]
            both.append(jnp.concatenate([one[:, :HALF_SPEC], one[:, HALF_SPEC:]], axis=0))
        hi, lo = split(jnp.concatenate(both, axis=1))
        spec = dot(plan.table(table_ref, "tap_rows"), jnp.concatenate([hi, hi, lo], axis=0))
        root_wide = jnp.sqrt(jnp.full((8, COL_LEN), weight_ref[0, k // 2], F32))
        root = root_wide[:1, :HALF_SPEC]
        for part in (k, k + 1):
            level_ref[part] = root_wide * sums[part : part + 1]
        out_ref[k] = spec[:, :HALF_SPEC] * root
        out_ref[k + 1] = spec[:, HALF_SPEC:] * root


def kernel_spectra(plan, kernels, socs_weight):
    count = kernels.shape[1] * kernels.shape[2]
    taps = kernels[0].transpose(0, 2, 1, 3)
    tables = plan.tap_packed
    hbm = pl.BlockSpec(memory_space=pltpu.HBM)
    return pl.pallas_call(
        functools.partial(spectra_body, plan),
        out_shape=(
            jax.ShapeDtypeStruct((count, 2 * plan.row_len, HALF_SPEC), F32),
            jax.ShapeDtypeStruct((count, 8, COL_LEN), F32),
        ),
        in_specs=[hbm] * 3,
        out_specs=(pl.BlockSpec(memory_space=pltpu.VMEM), pl.BlockSpec(memory_space=pltpu.VMEM)),
        scratch_shapes=[
            pltpu.SMEM(socs_weight.shape, F32),
            pltpu.VMEM(taps.shape, F32),
            pltpu.VMEM(tables.shape, BF),
            pltpu.SemaphoreType.DMA((3,)),
        ],
        compiler_params=pltpu.CompilerParams(vmem_limit_bytes=4 * 1024 * 1024),
        name="spectra",
    )(
        *(
            pltpu.with_memory_space_constraint(value, pltpu.HBM)
            for value in (socs_weight, taps, jnp.asarray(tables))
        ),
    )


def gradient_body(
    plan,
    dose_ref,
    mask_ref,
    target_ref,
    weight_ref,
    spec_ref,
    level_ref,
    table_ref,
    out_ref,
    s_ref,
    field_ref,
    light_ref,
    acc_ref,
    hold_ref,
    back_ref,
):
    tiles = plan.col_tiles
    rows = plan.row_len
    fr = plan.field_pad
    g = HALF_SPEC
    count = spec_ref.shape[0]

    along = []
    edges = plan.table(table_ref, "edges").astype(F32)
    for t in range(tiles):
        window = mask_ref[:, plan.starts[t] : plan.starts[t] + COL_LEN]
        a = dot(window, plan.table(table_ref, "col_fwd", t))
        if t == 0:
            a = a + (edges[0:1] + edges[1:2])
        if t == tiles - 1:
            a = a + (edges[2:3] + edges[3:4])
        along.append(jnp.concatenate([a[:, :g], a[:, g:]], axis=0).astype(BF))
    s_ref[...] = dot(plan.table(table_ref, "row_fwd"), jnp.concatenate(along, axis=1))
    light_ref[...] = jnp.zeros_like(light_ref)
    acc_ref[...] = jnp.zeros_like(acc_ref)
    chunks = [(at, at + CHUNK, at + 2 * CHUNK) for at in range(0, 2 * rows, 2 * CHUNK)]

    groups = count // GROUP

    def multiply(group):
        passed = []
        for t in range(tiles):
            lane = slice(t * g, t * g + g)
            prods = [[] for _ in range(GROUP)]
            for a, b, c in chunks:
                s_re, s_im = s_ref[a:b, lane].astype(BF), s_ref[b:c, lane].astype(BF)
                for part in range(GROUP):
                    k = GROUP * group + part
                    k_re, k_im = spec_ref[k, a:b].astype(BF), spec_ref[k, b:c].astype(BF)
                    prods[part].append(s_re * k_re - s_im * k_im)
                    prods[part].append(s_re * k_im + s_im * k_re)
            block = jnp.concatenate([jnp.concatenate(p, axis=0) for p in prods], axis=1)
            passed.append(dot(plan.table(table_ref, "row_inv"), block))
        stack = []
        for t in range(tiles):
            for part in range(GROUP):
                lane = slice(part * g, part * g + g)
                stack.append(jnp.concatenate([passed[t][:fr, lane], passed[t][fr:, lane]], axis=1))
        hold_ref[group % 2] = jnp.concatenate(stack, axis=0).astype(BF)

    def image(group):
        field = dot(hold_ref[group % 2], plan.table(table_ref, "col_inv"))
        for t in range(tiles):
            total = light_ref[t]
            for part in range(GROUP):
                at = (GROUP * t + part) * fr
                one = field[at : at + fr] + level_ref[GROUP * group + part, :1]
                field_ref[group, at : at + fr] = one
                total = total + one * one
            light_ref[t] = total

    def forward(group, carry):
        image(group)
        multiply(group + 1)
        return carry

    multiply(0)
    lax.fori_loop(0, groups - 1, forward, 0, unroll=True)
    image(groups - 1)

    dose = dose_ref[:1, :1]
    row = lax.broadcasted_iota(jnp.int32, (fr, COL_LEN), 0)
    col = lax.broadcasted_iota(jnp.int32, (fr, COL_LEN), 1)
    reach, strip = plan.reach, plan.strip_rows
    for t in range(tiles):
        lane = slice(plan.starts[t], plan.starts[t] + COL_LEN)
        resist = 1.0 / (1.0 + jnp.exp(-steep * (dose * light_ref[t] - thresh)))
        missed = resist - target_ref[:, lane].astype(F32)
        above, here, below = (weight_ref[i : i + 1, lane] for i in range(3))
        weight = jnp.where(row < reach, above, jnp.where(row < reach + strip, here, below))
        low, high = plan.bounds[t] - plan.starts[t], plan.bounds[t + 1] - plan.starts[t]
        kept = (row < plan.field_rows) & (col >= low) & (col < high)
        weight = jnp.where(kept, weight, 0.0)
        factor = 4.0 * loss_scale * steep * dose
        light_ref[t] = factor * weight * missed * resist * (1.0 - resist)

    def image_back(group):
        stack = []
        for t in range(tiles):
            for part in range(GROUP):
                at = (GROUP * t + part) * fr
                stack.append(light_ref[t] * field_ref[group, at : at + fr])
        inner = dot(jnp.concatenate(stack, axis=0).astype(BF), plan.table(table_ref, "col_inv_adj"))
        for t in range(tiles):
            block = []
            for part in range(GROUP):
                at = (GROUP * t + part) * fr
                d = inner[at : at + fr]
                block.append(jnp.concatenate([d[:, :g], d[:, g:]], axis=0))
            back_ref[group % 2, t] = jnp.concatenate(block, axis=1).astype(BF)

    def multiply_back(group):
        for t in range(tiles):
            lane = slice(t * g, t * g + g)
            d_prod = dot(plan.table(table_ref, "row_inv_adj"), back_ref[group % 2, t])
            for a, b, c in chunks:
                sum_re, sum_im = acc_ref[a:b, lane], acc_ref[b:c, lane]
                for part in range(GROUP):
                    k = GROUP * group + part
                    k_re, k_im = spec_ref[k, a:b], spec_ref[k, b:c]
                    at = slice(part * g, part * g + g)
                    d_re, d_im = d_prod[a:b, at], d_prod[b:c, at]
                    sum_re = sum_re + (d_re * k_re + d_im * k_im)
                    sum_im = sum_im + (d_im * k_re - d_re * k_im)
                acc_ref[a:b, lane] = sum_re
                acc_ref[b:c, lane] = sum_im

    def backward(group, carry):
        multiply_back(group)
        image_back(group + 1)
        return carry

    image_back(0)
    lax.fori_loop(0, groups - 1, backward, 0, unroll=True)
    multiply_back(groups - 1)

    d_along = dot(plan.table(table_ref, "row_adj"), acc_ref[...].astype(BF))
    parts = []
    for t in range(tiles):
        lane = slice(t * g, t * g + g)
        both = jnp.concatenate([d_along[:strip, lane], d_along[strip:, lane]], axis=1).astype(BF)
        parts.append(dot(both, plan.table(table_ref, "col_adj", t)))
    blocks = []
    for b in range(plan.width // LANES):
        terms = []
        for t in range(tiles):
            at = b * LANES - plan.starts[t]
            if 0 <= at < COL_LEN:
                terms.append(parts[t][:, at : at + LANES])
        blocks.append(functools.reduce(lambda x, y: x + y, terms))
    out_ref[...] = jnp.concatenate(blocks, axis=1)


def strip_gradient(plan, mask_ext, target_ext, weights, spec, dose, tables):
    vmem = pl.BlockSpec(memory_space=pltpu.VMEM)
    count = spec[0].shape[0]
    spectrum = (2 * plan.row_len, plan.col_tiles * HALF_SPEC)
    image = (plan.col_tiles, plan.field_pad, COL_LEN)
    return pl.pallas_call(
        functools.partial(gradient_body, plan),
        out_shape=jax.ShapeDtypeStruct((plan.strip_rows, plan.width), F32),
        in_specs=[vmem] * 7,
        out_specs=vmem,
        scratch_shapes=[
            pltpu.VMEM(spectrum, F32),
            pltpu.VMEM((count // GROUP, GROUP * plan.col_tiles * plan.field_pad, COL_LEN), F32),
            pltpu.VMEM(image, F32),
            pltpu.VMEM(spectrum, F32),
            pltpu.VMEM((2, GROUP * plan.col_tiles * plan.field_pad, COL_LEN), BF),
            pltpu.VMEM((2, plan.col_tiles, 2 * plan.field_pad, GROUP * HALF_SPEC), BF),
        ],
        compiler_params=pltpu.CompilerParams(vmem_limit_bytes=12 * 1024 * 1024),
        name="gradient",
    )(dose, mask_ext, target_ext, weights, *spec, tables)


def other_corner(value):
    return lax.ppermute(value, "corner", [(0, 1), (1, 0)])


def neighbours(flags, top, bottom, blank):
    strips = lax.axis_size("tile")
    first_corner, highest, lowest = flags
    cycle = [(2 * i, 2 * i + 2) for i in range(strips - 1)] + [(2 * strips - 2, 2 * strips - 1)]
    cycle += [(2 * i + 1, 2 * i - 1) for i in range(1, strips)] + [(1, 0)]
    message = jnp.where(first_corner, bottom, top)
    got = lax.ppermute(message, ("tile", "corner"), cycle)
    shared = other_corner(got)
    above = jnp.where(highest, blank, jnp.where(first_corner, got, shared))
    below = jnp.where(lowest, blank, jnp.where(first_corner, shared, got))
    return above, below


def per_device(
    mask_logits, target, adam_first, adam_second, tile_counts, kernels, socs_weight, corner_dose
):
    strip_rows, half_width = mask_logits.shape
    width = target.shape[1]
    plan = plan_of(strip_rows, width, kernels.shape[-1])
    reach = plan.reach
    halo = 2 * reach

    def whole(own, other):
        left = jnp.where(first_corner, own, other)
        right = jnp.where(first_corner, other, own)
        return jnp.concatenate([left, right], axis=-1)

    def own_half(value):
        return jnp.where(first_corner, value[..., :half_width], value[..., half_width:])

    def extended(above_rows, own, below_rows, total):
        have = above_rows.shape[0] + own.shape[0] + below_rows.shape[0]
        blank = jnp.zeros((total - have, own.shape[1]), own.dtype)
        return jnp.concatenate([above_rows, own, below_rows, blank], axis=0)

    tables = jnp.asarray(plan.packed)

    mask_half, state, target, counts, facts = fetch(
        mask_logits, adam_first, adam_second, target, tile_counts
    )
    flags = [facts[i, :1, :1] > 0.5 for i in range(3)]
    first_corner = flags[0]
    dose = jnp.broadcast_to(corner_dose[None], (8, LANES))
    counts = counts[:1]
    counts_bf = counts.astype(BF)
    other_half = other_corner(mask_half)
    mask_bf = whole(mask_half, other_half)
    above, below = neighbours(
        flags,
        jnp.concatenate([mask_bf[:halo], target[:reach], counts_bf], axis=0),
        jnp.concatenate([mask_bf[-halo:], target[-reach:], counts_bf], axis=0),
        jnp.where(jnp.arange(halo + reach + 1)[:, None] < halo, -MIDDLE, 0.0).astype(BF),
    )
    spec = kernel_spectra(plan, kernels, socs_weight)
    target_ext = extended(
        above[halo : halo + reach], target, below[halo : halo + reach], plan.field_pad
    )
    near = jnp.concatenate(
        [above[halo + reach :].astype(F32), counts, below[halo + reach :].astype(F32)]
    )
    near = jnp.pad(near, ((0, 5), (0, 0)))
    weights = near / (near + 4.0)
    above, below = above[:halo], below[:halo]
    mask_ext = extended(above, mask_bf, below, plan.row_len)
    state = whole(state, other_corner(state))
    partial = strip_gradient(plan, mask_ext, target_ext, weights, spec, dose, tables)

    logits, first, second = state[0], state[1], state[2]
    opacity = jax.nn.sigmoid(logits)
    for iteration in range(ITERS):
        if iteration:
            opacity = jax.nn.sigmoid(logits)
            mask_bf = (lax.reduce_precision(opacity, 8, 7) - MIDDLE).astype(BF)
            blank = jnp.full((halo, 1), -MIDDLE, BF)
            above, below = neighbours(flags, mask_bf[:halo], mask_bf[-halo:], blank)
            mask_ext = extended(above, mask_bf, below, plan.row_len)
            partial = strip_gradient(plan, mask_ext, target_ext, weights, spec, dose, tables)
        if iteration < ITERS - 1:
            summed = partial + other_corner(partial.astype(BF)).astype(F32)
        else:
            mine = own_half(partial)
            theirs = jnp.where(first_corner, partial[:, half_width:], partial[:, :half_width])
            summed = mine + other_corner(theirs.astype(BF)).astype(F32)
            opacity, logits = own_half(opacity), own_half(logits)
            first, second = own_half(first), own_half(second)
        gradient = summed * opacity * (1.0 - opacity)
        count_now = prior_steps + iteration + 1.0
        first = beta_one * first + (1.0 - beta_one) * gradient
        second = beta_two * second + (1.0 - beta_two) * gradient * gradient
        first_hat = first / (1.0 - beta_one**count_now)
        second_hat = second / (1.0 - beta_two**count_now)
        logits = logits - step_size * first_hat / (jnp.sqrt(second_hat) + adam_eps)
    return (logits, first, second)


def solution(mesh):
    return jax.shard_map(
        per_device,
        mesh=mesh,
        in_specs=(
            P(("grp", "tile"), "corner"),
            P(("grp", "tile"), None),
            P(("grp", "tile"), "corner"),
            P(("grp", "tile"), "corner"),
            P(("grp", "tile"), None),
            P("corner", None, None, None, None),
            P("corner", None),
            P("corner"),
        ),
        out_specs=(
            P(("grp", "tile"), "corner"),
            P(("grp", "tile"), "corner"),
            P(("grp", "tile"), "corner"),
        ),
        check_vma=False,
    )
```

```python
import functools
import math

import jax
import jax.numpy as jnp
import numpy as np
from jax import lax
from jax.experimental import pallas as pl
from jax.experimental.pallas import tpu as pltpu
from jax.sharding import PartitionSpec as P


ITERS = 2

steep = 8.0
thresh = 0.5
loss_scale = 20.0
step_size = 0.05
beta_one = 0.9
beta_two = 0.999
adam_eps = 1e-08
prior_steps = 1000.0

LANES = 128
HALF_SPEC = 128
MIDDLE = 0.5
COL_LEN = 2 * HALF_SPEC
CHUNK = 16
GROUP = 2

BF = jnp.bfloat16
F32 = jnp.float32


def up_to(value, unit):
    return -(-value // unit) * unit


class Plan:
    def __init__(self, strip_rows, width, taps):
        reach = taps // 2
        self.strip_rows, self.width, self.taps, self.reach = strip_rows, width, taps, reach
        self.field_rows = strip_rows + 2 * reach
        self.field_pad = up_to(self.field_rows, 8)
        self.ext_rows = strip_rows + 4 * reach
        self.row_len = up_to(self.ext_rows, 128)
        self.taps_pad = up_to(taps, 8)
        self.col_tiles = width // LANES - 1
        self.starts = [LANES * t for t in range(self.col_tiles)]
        assert width % LANES == 0 and self.col_tiles >= 2
        assert LANES > 4 * reach
        edge = LANES // 2 - 8
        self.bounds = [0] + [s + edge for s in self.starts[1:]] + [width]

        omega = 2.0 * math.pi * (np.arange(HALF_SPEC) + 0.5) / COL_LEN
        phi = 2.0 * math.pi * np.arange(self.row_len) / self.row_len
        rows = np.arange(self.row_len)

        fwd = []
        for t, start in enumerate(self.starts):
            x = start + np.arange(COL_LEN)
            keep = np.ones(COL_LEN)
            if t == 0:
                keep = keep * (x < COL_LEN - reach)
            if t == self.col_tiles - 1:
                keep = keep * (x >= start + reach)
            angle = (x - start)[:, None] * omega[None, :]
            fwd.append(np.concatenate([np.cos(angle), -np.sin(angle)], 1) * keep[:, None])
        self.col_fwd = np.stack(fwd)
        edges = []
        for x in (np.arange(-reach, 0), COL_LEN + np.arange(reach)):
            angle = x[:, None] * omega[None, :]
            edge = -MIDDLE * np.concatenate([np.cos(angle), -np.sin(angle)], 1).sum(0)
            edges += split_table(edge)
        self.edges = np.stack(edges)
        self.col_adj = self.col_fwd.transpose(0, 2, 1)

        scale = 2.0 / (COL_LEN * self.row_len)
        angle = omega[:, None] * np.arange(COL_LEN)[None, :]
        self.col_inv = np.concatenate([np.cos(angle), -np.sin(angle)], 0) * scale
        self.col_inv_adj = self.col_inv.T

        angle = phi[:, None] * rows[None, :]
        live = (rows < self.ext_rows)[None, :]
        c, s = np.cos(angle) * live, np.sin(angle) * live
        mixed = np.arange(2 * self.row_len).reshape(2, -1, CHUNK).transpose(1, 0, 2).reshape(-1)
        self.row_fwd = np.block([[c, s], [-s, c]])[mixed]
        own = slice(2 * reach, 2 * reach + strip_rows)
        self.row_adj = np.block([[c[:, own].T, -s[:, own].T], [s[:, own].T, c[:, own].T]])[:, mixed]

        angle = (np.arange(self.field_pad) + reach)[:, None] * phi[None, :]
        live = (np.arange(self.field_pad) < self.field_rows)[:, None]
        c, s = np.cos(angle) * live, np.sin(angle) * live
        self.row_inv = np.block([[c, -s], [s, c]])[:, mixed]
        self.row_inv_adj = self.row_inv.T

        tap = np.arange(taps) - reach
        angle = tap[:, None] * omega[None, :]
        self.tap_cols = np.concatenate([np.cos(angle), -np.sin(angle)], 1)
        angle = phi[:, None] * tap[None, :]
        fill = ((0, 0), (0, self.taps_pad - taps))
        c, s = np.pad(np.cos(angle), fill), np.pad(np.sin(angle), fill)
        self.tap_rows = np.block([[c, s], [-s, c]])[mixed]


        rows_hi, rows_lo = split_table(self.tap_rows)
        cols_hi, cols_lo = split_table(self.tap_cols)
        parts = {
            "col_fwd": self.col_fwd.reshape(-1, COL_LEN),
            "col_adj": self.col_adj.reshape(-1, COL_LEN),
            "col_inv": self.col_inv,
            "col_inv_adj": self.col_inv_adj,
            "row_fwd": self.row_fwd,
            "row_adj": self.row_adj,
            "row_inv": self.row_inv,
            "row_inv_adj": self.row_inv_adj,
            "edges": self.edges,
        }
        tap_parts = {
            "tap_rows": np.concatenate([rows_hi, rows_lo, rows_hi], axis=1),
            "tap_hi": cols_hi,
            "tap_lo": cols_lo,
        }
        self.where = {}
        self.packed = self.pack(parts)
        self.tap_packed = self.pack(tap_parts)

    def pack(self, parts):
        packed, at = [], 0
        wide = max(part.shape[1] for part in parts.values())
        for name, part in parts.items():
            part = np.asarray(part, np.float32).astype(BF)
            self.where[name] = (at, part.shape[0], part.shape[1])
            fill = up_to(part.shape[0], CHUNK) - part.shape[0]
            packed.append(np.pad(part, ((0, fill), (0, wide - part.shape[1]))))
            at += part.shape[0] + fill
        return np.concatenate(packed, axis=0)

    def table(self, ref, name, block=None):
        at, rows, cols = self.where[name]
        if block is not None:
            at, rows = at + block * COL_LEN, COL_LEN
        return ref[at : at + rows, :cols]


@functools.lru_cache(maxsize=None)
def plan_of(strip_rows, width, taps):
    return Plan(strip_rows, width, taps)


def split_table(table):
    high = np.asarray(table, np.float32).astype(BF)
    low = (np.asarray(table, np.float64) - high.astype(np.float64)).astype(np.float32).astype(BF)
    return high, low


def dot(left, right):
    return lax.dot_general(left, right, (((1,), (0,)), ((), ())), preferred_element_type=F32)


def split(value):
    high = value.astype(BF)
    return high, (value - high.astype(F32)).astype(BF)


def fetch_body(
    logits_hbm,
    first_hbm,
    second_hbm,
    target_hbm,
    counts_hbm,
    taps_hbm,
    tables_hbm,
    socs_hbm,
    mask_ref,
    state_ref,
    target_ref,
    counts_ref,
    flags_ref,
    taps_ref,
    tables_ref,
    roots_ref,
    counts_smem,
    socs_smem,
    sems,
):
    pairs = (
        (logits_hbm, state_ref.at[0]),
        (counts_hbm, counts_smem),
        (target_hbm, target_ref),
        (first_hbm, state_ref.at[1]),
        (second_hbm, state_ref.at[2]),
        (taps_hbm, taps_ref),
        (tables_hbm, tables_ref),
        (socs_hbm, socs_smem),
    )
    copies = [pltpu.make_async_copy(a, b, sems.at[i]) for i, (a, b) in enumerate(pairs)]
    for copy in copies:
        copy.start()
    place, corner = lax.axis_index("tile"), lax.axis_index("corner")
    facts = (corner == 0, place == 0, place == lax.axis_size("tile") - 1)
    for i, fact in enumerate(facts):
        flags_ref[i] = jnp.full(flags_ref.shape[1:], jnp.where(fact, 1.0, 0.0), F32)
    copies[0].wait()
    mask = (1.0 / (1.0 + jnp.exp(-state_ref[0]))).astype(BF)
    mask_ref[...] = (mask.astype(F32) - MIDDLE).astype(BF)
    for copy in copies[1:]:
        copy.wait()
    for k in range(roots_ref.shape[0]):
        roots_ref[k] = jnp.sqrt(jnp.full(roots_ref.shape[1:], socs_smem[0, k], F32))
    tiles = counts_smem.shape[1]
    wide = counts_ref.shape[1] // tiles
    for tile in range(tiles):
        value = counts_smem[0, tile].astype(F32)
        counts_ref[:, tile * wide : (tile + 1) * wide] = jnp.full((8, wide), value, F32)


def fetch(
    flag_rows, mask_logits, adam_first, adam_second, target, tile_counts, taps, tables, socs_weight
):
    args = (
        mask_logits, adam_first, adam_second, target, tile_counts, taps, tables, socs_weight
    )
    shape = mask_logits.shape
    outs = (
        jax.ShapeDtypeStruct(shape, BF),
        jax.ShapeDtypeStruct((3,) + shape, F32),
        jax.ShapeDtypeStruct(target.shape, BF),
        jax.ShapeDtypeStruct((8, target.shape[1]), F32),
        jax.ShapeDtypeStruct((3, flag_rows, target.shape[1]), F32),
        jax.ShapeDtypeStruct(taps.shape, F32),
        jax.ShapeDtypeStruct(tables.shape, BF),
        jax.ShapeDtypeStruct((socs_weight.shape[1], 8, COL_LEN), F32),
    )
    return pl.pallas_call(
        fetch_body,
        out_shape=outs,
        in_specs=[pl.BlockSpec(memory_space=pltpu.HBM)] * len(args),
        out_specs=tuple(pl.BlockSpec(memory_space=pltpu.VMEM) for _ in outs),
        scratch_shapes=[
            pltpu.SMEM(tile_counts.shape, jnp.int32),
            pltpu.SMEM(socs_weight.shape, F32),
            pltpu.SemaphoreType.DMA((len(args),)),
        ],
        compiler_params=pltpu.CompilerParams(vmem_limit_bytes=4 * 1024 * 1024),
        name="fetch",
    )(*(pltpu.with_memory_space_constraint(value, pltpu.HBM) for value in args))


def spectra_body(plan, root_ref, kern_ref, table_ref, out_ref, level_ref):
    count = out_ref.shape[0]
    pad = plan.taps_pad - plan.taps
    stack, sums = [], []
    for k in range(count):
        taps = kern_ref[k // 2, :, k % 2, :]
        sums.append(jnp.sum(taps, axis=0, keepdims=True))
        stack.append(jnp.concatenate([taps, jnp.zeros((pad, plan.taps), F32)], axis=0))
    hi, lo = split(jnp.concatenate(stack, axis=0))
    sums = MIDDLE * jnp.sum(jnp.concatenate(sums, axis=0), axis=1, keepdims=True)
    sums = jnp.broadcast_to(sums, (count, COL_LEN))
    cols_hi, cols_lo = plan.table(table_ref, "tap_hi"), plan.table(table_ref, "tap_lo")
    half = dot(hi, cols_hi) + dot(lo, cols_hi) + dot(hi, cols_lo)
    for k in range(0, count, 2):
        both = []
        for part in (k, k + 1):
            one = half[part * plan.taps_pad : (part + 1) * plan.taps_pad]
            both.append(jnp.concatenate([one[:, :HALF_SPEC], one[:, HALF_SPEC:]], axis=0))
        hi, lo = split(jnp.concatenate(both, axis=1))
        spec = dot(plan.table(table_ref, "tap_rows"), jnp.concatenate([hi, hi, lo], axis=0))
        root_wide = root_ref[k // 2]
        root = root_wide[:1, :HALF_SPEC]
        for part in (k, k + 1):
            level_ref[part] = root_wide * sums[part : part + 1]
        out_ref[k] = spec[:, :HALF_SPEC] * root
        out_ref[k + 1] = spec[:, HALF_SPEC:] * root


def kernel_spectra(plan, taps, tables, roots):
    count = 2 * taps.shape[0]
    vmem = pl.BlockSpec(memory_space=pltpu.VMEM)
    return pl.pallas_call(
        functools.partial(spectra_body, plan),
        out_shape=(
            jax.ShapeDtypeStruct((count, 2 * plan.row_len, HALF_SPEC), F32),
            jax.ShapeDtypeStruct((count, 8, COL_LEN), F32),
        ),
        in_specs=[vmem] * 3,
        out_specs=(vmem, vmem),
        compiler_params=pltpu.CompilerParams(vmem_limit_bytes=4 * 1024 * 1024),
        name="spectra",
    )(roots, taps, tables)


def gradient_body(
    plan,
    dose_ref,
    mask_ref,
    target_ref,
    weight_ref,
    spec_ref,
    level_ref,
    table_ref,
    out_ref,
    s_ref,
    field_ref,
    light_ref,
    acc_ref,
    hold_ref,
    back_ref,
):
    tiles = plan.col_tiles
    rows = plan.row_len
    fr = plan.field_pad
    g = HALF_SPEC
    count = spec_ref.shape[0]

    along = []
    edges = plan.table(table_ref, "edges").astype(F32)
    for t in range(tiles):
        window = mask_ref[:, plan.starts[t] : plan.starts[t] + COL_LEN]
        a = dot(window, plan.table(table_ref, "col_fwd", t))
        if t == 0:
            a = a + (edges[0:1] + edges[1:2])
        if t == tiles - 1:
            a = a + (edges[2:3] + edges[3:4])
        along.append(jnp.concatenate([a[:, :g], a[:, g:]], axis=0).astype(BF))
    s_ref[...] = dot(plan.table(table_ref, "row_fwd"), jnp.concatenate(along, axis=1))
    light_ref[...] = jnp.zeros_like(light_ref)
    acc_ref[...] = jnp.zeros_like(acc_ref)
    chunks = [(at, at + CHUNK, at + 2 * CHUNK) for at in range(0, 2 * rows, 2 * CHUNK)]

    groups = count // GROUP

    def multiply(group):
        passed = []
        for t in range(tiles):
            lane = slice(t * g, t * g + g)
            prods = [[] for _ in range(GROUP)]
            for a, b, c in chunks:
                s_re, s_im = s_ref[a:b, lane].astype(BF), s_ref[b:c, lane].astype(BF)
                for part in range(GROUP):
                    k = GROUP * group + part
                    k_re, k_im = spec_ref[k, a:b].astype(BF), spec_ref[k, b:c].astype(BF)
                    prods[part].append(s_re * k_re - s_im * k_im)
                    prods[part].append(s_re * k_im + s_im * k_re)
            block = jnp.concatenate([jnp.concatenate(p, axis=0) for p in prods], axis=1)
            passed.append(dot(plan.table(table_ref, "row_inv"), block))
        stack = []
        for t in range(tiles):
            for part in range(GROUP):
                lane = slice(part * g, part * g + g)
                stack.append(jnp.concatenate([passed[t][:fr, lane], passed[t][fr:, lane]], axis=1))
        hold_ref[group % 2] = jnp.concatenate(stack, axis=0).astype(BF)

    def image(group):
        field = dot(hold_ref[group % 2], plan.table(table_ref, "col_inv"))
        for t in range(tiles):
            total = light_ref[t]
            for part in range(GROUP):
                at = (GROUP * t + part) * fr
                one = field[at : at + fr] + level_ref[GROUP * group + part, :1]
                field_ref[group, at : at + fr] = one
                total = total + one * one
            light_ref[t] = total

    def forward(group, carry):
        image(group)
        multiply(group + 1)
        return carry

    multiply(0)
    lax.fori_loop(0, groups - 1, forward, 0, unroll=True)
    image(groups - 1)

    dose = dose_ref[:1, :1]
    row = lax.broadcasted_iota(jnp.int32, (fr, COL_LEN), 0)
    col = lax.broadcasted_iota(jnp.int32, (fr, COL_LEN), 1)
    reach, strip = plan.reach, plan.strip_rows
    for t in range(tiles):
        lane = slice(plan.starts[t], plan.starts[t] + COL_LEN)
        resist = 1.0 / (1.0 + jnp.exp(-steep * (dose * light_ref[t] - thresh)))
        missed = resist - target_ref[:, lane].astype(F32)
        above, here, below = (weight_ref[i : i + 1, lane] for i in range(3))
        weight = jnp.where(row < reach, above, jnp.where(row < reach + strip, here, below))
        low, high = plan.bounds[t] - plan.starts[t], plan.bounds[t + 1] - plan.starts[t]
        kept = (row < plan.field_rows) & (col >= low) & (col < high)
        weight = jnp.where(kept, weight, 0.0)
        factor = 4.0 * loss_scale * steep * dose
        light_ref[t] = factor * weight * missed * resist * (1.0 - resist)

    def image_back(group):
        stack = []
        for t in range(tiles):
            for part in range(GROUP):
                at = (GROUP * t + part) * fr
                stack.append(light_ref[t] * field_ref[group, at : at + fr])
        inner = dot(jnp.concatenate(stack, axis=0).astype(BF), plan.table(table_ref, "col_inv_adj"))
        for t in range(tiles):
            block = []
            for part in range(GROUP):
                at = (GROUP * t + part) * fr
                d = inner[at : at + fr]
                block.append(jnp.concatenate([d[:, :g], d[:, g:]], axis=0))
            back_ref[group % 2, t] = jnp.concatenate(block, axis=1).astype(BF)

    def multiply_back(group):
        for t in range(tiles):
            lane = slice(t * g, t * g + g)
            d_prod = dot(plan.table(table_ref, "row_inv_adj"), back_ref[group % 2, t])
            for a, b, c in chunks:
                sum_re, sum_im = acc_ref[a:b, lane], acc_ref[b:c, lane]
                for part in range(GROUP):
                    k = GROUP * group + part
                    k_re, k_im = spec_ref[k, a:b], spec_ref[k, b:c]
                    at = slice(part * g, part * g + g)
                    d_re, d_im = d_prod[a:b, at], d_prod[b:c, at]
                    sum_re = sum_re + (d_re * k_re + d_im * k_im)
                    sum_im = sum_im + (d_im * k_re - d_re * k_im)
                acc_ref[a:b, lane] = sum_re
                acc_ref[b:c, lane] = sum_im

    def backward(group, carry):
        multiply_back(group)
        image_back(group + 1)
        return carry

    image_back(0)
    lax.fori_loop(0, groups - 1, backward, 0, unroll=True)
    multiply_back(groups - 1)

    d_along = dot(plan.table(table_ref, "row_adj"), acc_ref[...].astype(BF))
    parts = []
    for t in range(tiles):
        lane = slice(t * g, t * g + g)
        both = jnp.concatenate([d_along[:strip, lane], d_along[strip:, lane]], axis=1).astype(BF)
        parts.append(dot(both, plan.table(table_ref, "col_adj", t)))
    blocks = []
    for b in range(plan.width // LANES):
        terms = []
        for t in range(tiles):
            at = b * LANES - plan.starts[t]
            if 0 <= at < COL_LEN:
                terms.append(parts[t][:, at : at + LANES])
        blocks.append(functools.reduce(lambda x, y: x + y, terms))
    out_ref[...] = jnp.concatenate(blocks, axis=1)


def strip_gradient(plan, mask_ext, target_ext, weights, spec, dose, tables):
    vmem = pl.BlockSpec(memory_space=pltpu.VMEM)
    count = spec[0].shape[0]
    spectrum = (2 * plan.row_len, plan.col_tiles * HALF_SPEC)
    image = (plan.col_tiles, plan.field_pad, COL_LEN)
    return pl.pallas_call(
        functools.partial(gradient_body, plan),
        out_shape=jax.ShapeDtypeStruct((plan.strip_rows, plan.width), F32),
        in_specs=[vmem] * 7,
        out_specs=vmem,
        scratch_shapes=[
            pltpu.VMEM(spectrum, F32),
            pltpu.VMEM((count // GROUP, GROUP * plan.col_tiles * plan.field_pad, COL_LEN), F32),
            pltpu.VMEM(image, F32),
            pltpu.VMEM(spectrum, F32),
            pltpu.VMEM((2, GROUP * plan.col_tiles * plan.field_pad, COL_LEN), BF),
            pltpu.VMEM((2, plan.col_tiles, 2 * plan.field_pad, GROUP * HALF_SPEC), BF),
        ],
        compiler_params=pltpu.CompilerParams(vmem_limit_bytes=12 * 1024 * 1024),
        name="gradient",
    )(dose, mask_ext, target_ext, weights, *spec, tables)


def other_corner(value):
    return lax.ppermute(value, "corner", [(0, 1), (1, 0)])


def neighbours(flags, top, bottom, blank):
    strips = lax.axis_size("tile")
    first_corner, highest, lowest = flags[:, : top.shape[0], : top.shape[1]]
    cycle = [(2 * i, 2 * i + 2) for i in range(strips - 1)] + [(2 * strips - 2, 2 * strips - 1)]
    cycle += [(2 * i + 1, 2 * i - 1) for i in range(1, strips)] + [(1, 0)]
    message = jnp.where(first_corner, bottom, top)
    got = lax.ppermute(message, ("tile", "corner"), cycle)
    shared = other_corner(got)
    above = jnp.where(highest, blank, jnp.where(first_corner, got, shared))
    below = jnp.where(lowest, blank, jnp.where(first_corner, shared, got))
    return above, below


def per_device(
    mask_logits, target, adam_first, adam_second, tile_counts, kernels, socs_weight, corner_dose
):
    strip_rows, half_width = mask_logits.shape
    width = target.shape[1]
    plan = plan_of(strip_rows, width, kernels.shape[-1])
    reach = plan.reach
    halo = 2 * reach

    def whole(own, other):
        first_corner = flags[0, : own.shape[-2], : own.shape[-1]]
        left = jnp.where(first_corner, own, other)
        right = jnp.where(first_corner, other, own)
        return jnp.concatenate([left, right], axis=-1)

    def own_half(value):
        first_corner = flags[0, : value.shape[-2], :half_width]
        return jnp.where(first_corner, value[..., :half_width], value[..., half_width:])

    def extended(above_rows, own, below_rows, total):
        have = above_rows.shape[0] + own.shape[0] + below_rows.shape[0]
        blank = jnp.zeros((total - have, own.shape[1]), own.dtype)
        return jnp.concatenate([above_rows, own, below_rows, blank], axis=0)

    tables = jnp.asarray(plan.packed)

    mask_half, state, target, counts, facts, taps, tap_tables, roots = fetch(
        up_to(max(strip_rows, halo + reach + 1), 8),
        mask_logits,
        adam_first,
        adam_second,
        target,
        tile_counts,
        kernels[0].transpose(0, 2, 1, 3),
        jnp.asarray(plan.tap_packed),
        socs_weight,
    )
    flags = facts > 0.5
    dose = jnp.broadcast_to(corner_dose[None], (8, LANES))
    counts = counts[:1]
    counts_bf = counts.astype(BF)
    other_half = other_corner(mask_half)
    mask_bf = whole(mask_half, other_half)
    above, below = neighbours(
        flags,
        jnp.concatenate([mask_bf[:halo], target[:reach], counts_bf], axis=0),
        jnp.concatenate([mask_bf[-halo:], target[-reach:], counts_bf], axis=0),
        jnp.where(jnp.arange(halo + reach + 1)[:, None] < halo, -MIDDLE, 0.0).astype(BF),
    )
    spec = kernel_spectra(plan, taps, tap_tables, roots)
    target_ext = extended(
        above[halo : halo + reach], target, below[halo : halo + reach], plan.field_pad
    )
    near = jnp.concatenate(
        [above[halo + reach :].astype(F32), counts, below[halo + reach :].astype(F32)]
    )
    near = jnp.pad(near, ((0, 5), (0, 0)))
    weights = near / (near + 4.0)
    above, below = above[:halo], below[:halo]
    mask_ext = extended(above, mask_bf, below, plan.row_len)
    state = whole(state, other_corner(state))
    partial = strip_gradient(plan, mask_ext, target_ext, weights, spec, dose, tables)

    logits, first, second = state[0], state[1], state[2]
    opacity = jax.nn.sigmoid(logits)
    for iteration in range(ITERS):
        if iteration:
            opacity = jax.nn.sigmoid(logits)
            mask_bf = (lax.reduce_precision(opacity, 8, 7) - MIDDLE).astype(BF)
            blank = jnp.full((halo, 1), -MIDDLE, BF)
            above, below = neighbours(flags, mask_bf[:halo], mask_bf[-halo:], blank)
            mask_ext = extended(above, mask_bf, below, plan.row_len)
            partial = strip_gradient(plan, mask_ext, target_ext, weights, spec, dose, tables)
        if iteration < ITERS - 1:
            summed = partial + other_corner(partial.astype(BF)).astype(F32)
        else:
            mine = own_half(partial)
            theirs = jnp.where(flags[0, :strip_rows, :half_width], partial[:, half_width:], partial[:, :half_width])
            summed = mine + other_corner(theirs.astype(BF)).astype(F32)
            opacity, logits = own_half(opacity), own_half(logits)
            first, second = own_half(first), own_half(second)
        gradient = summed * opacity * (1.0 - opacity)
        count_now = prior_steps + iteration + 1.0
        first = beta_one * first + (1.0 - beta_one) * gradient
        second = beta_two * second + (1.0 - beta_two) * gradient * gradient
        first_hat = first / (1.0 - beta_one**count_now)
        second_hat = second / (1.0 - beta_two**count_now)
        logits = logits - step_size * first_hat / (jnp.sqrt(second_hat) + adam_eps)
    return (logits, first, second)


def solution(mesh):
    return jax.shard_map(
        per_device,
        mesh=mesh,
        in_specs=(
            P(("grp", "tile"), "corner"),
            P(("grp", "tile"), None),
            P(("grp", "tile"), "corner"),
            P(("grp", "tile"), "corner"),
            P(("grp", "tile"), None),
            P("corner", None, None, None, None),
            P("corner", None),
            P("corner"),
        ),
        out_specs=(
            P(("grp", "tile"), "corner"),
            P(("grp", "tile"), "corner"),
            P(("grp", "tile"), "corner"),
        ),
        check_vma=False,
    )
```

```python
import functools
import math

import jax
import jax.numpy as jnp
import numpy as np
from jax import lax
from jax.experimental import pallas as pl
from jax.experimental.pallas import tpu as pltpu
from jax.sharding import PartitionSpec as P


ITERS = 2

steep = 8.0
thresh = 0.5
loss_scale = 20.0
step_size = 0.05
beta_one = 0.9
beta_two = 0.999
adam_eps = 1e-08
prior_steps = 1000.0

LANES = 128
HALF_SPEC = 128
MIDDLE = 0.5
COL_LEN = 2 * HALF_SPEC
CHUNK = 16
GROUP = 4

BF = jnp.bfloat16
F32 = jnp.float32


def up_to(value, unit):
    return -(-value // unit) * unit


class Plan:
    def __init__(self, strip_rows, width, taps):
        reach = taps // 2
        self.strip_rows, self.width, self.taps, self.reach = strip_rows, width, taps, reach
        self.field_rows = strip_rows + 2 * reach
        self.field_pad = up_to(self.field_rows, 8)
        self.ext_rows = strip_rows + 4 * reach
        self.row_len = up_to(self.ext_rows, 128)
        self.taps_pad = up_to(taps, 8)
        self.col_tiles = width // LANES - 1
        self.starts = [LANES * t for t in range(self.col_tiles)]
        assert width % LANES == 0 and self.col_tiles >= 2
        assert LANES > 4 * reach
        edge = LANES // 2 - 8
        self.bounds = [0] + [s + edge for s in self.starts[1:]] + [width]

        omega = 2.0 * math.pi * (np.arange(HALF_SPEC) + 0.5) / COL_LEN
        phi = 2.0 * math.pi * np.arange(self.row_len) / self.row_len
        rows = np.arange(self.row_len)

        fwd = []
        for t, start in enumerate(self.starts):
            x = start + np.arange(COL_LEN)
            keep = np.ones(COL_LEN)
            if t == 0:
                keep = keep * (x < COL_LEN - reach)
            if t == self.col_tiles - 1:
                keep = keep * (x >= start + reach)
            angle = (x - start)[:, None] * omega[None, :]
            fwd.append(np.concatenate([np.cos(angle), -np.sin(angle)], 1) * keep[:, None])
        self.col_fwd = np.stack(fwd)
        edges = []
        for x in (np.arange(-reach, 0), COL_LEN + np.arange(reach)):
            angle = x[:, None] * omega[None, :]
            edge = -MIDDLE * np.concatenate([np.cos(angle), -np.sin(angle)], 1).sum(0)
            edges += split_table(edge)
        self.edges = np.stack(edges)
        self.col_adj = self.col_fwd.transpose(0, 2, 1)

        scale = 2.0 / (COL_LEN * self.row_len)
        angle = omega[:, None] * np.arange(COL_LEN)[None, :]
        self.col_inv = np.concatenate([np.cos(angle), -np.sin(angle)], 0) * scale
        self.col_inv_adj = self.col_inv.T

        angle = phi[:, None] * rows[None, :]
        live = (rows < self.ext_rows)[None, :]
        c, s = np.cos(angle) * live, np.sin(angle) * live
        mixed = np.arange(2 * self.row_len).reshape(2, -1, CHUNK).transpose(1, 0, 2).reshape(-1)
        self.row_fwd = np.block([[c, s], [-s, c]])[mixed]
        own = slice(2 * reach, 2 * reach + strip_rows)
        self.row_adj = np.block([[c[:, own].T, -s[:, own].T], [s[:, own].T, c[:, own].T]])[:, mixed]

        angle = (np.arange(self.field_pad) + reach)[:, None] * phi[None, :]
        live = (np.arange(self.field_pad) < self.field_rows)[:, None]
        c, s = np.cos(angle) * live, np.sin(angle) * live
        self.row_inv = np.block([[c, -s], [s, c]])[:, mixed]
        self.row_inv_adj = self.row_inv.T

        tap = np.arange(taps) - reach
        angle = tap[:, None] * omega[None, :]
        self.tap_cols = np.concatenate([np.cos(angle), -np.sin(angle)], 1)
        angle = phi[:, None] * tap[None, :]
        fill = ((0, 0), (0, self.taps_pad - taps))
        c, s = np.pad(np.cos(angle), fill), np.pad(np.sin(angle), fill)
        self.tap_rows = np.block([[c, s], [-s, c]])[mixed]


        rows_hi, rows_lo = split_table(self.tap_rows)
        cols_hi, cols_lo = split_table(self.tap_cols)
        parts = {
            "col_fwd": self.col_fwd.reshape(-1, COL_LEN),
            "col_adj": self.col_adj.reshape(-1, COL_LEN),
            "col_inv": self.col_inv,
            "col_inv_adj": self.col_inv_adj,
            "row_fwd": self.row_fwd,
            "row_adj": self.row_adj,
            "row_inv": self.row_inv,
            "row_inv_adj": self.row_inv_adj,
            "edges": self.edges,
        }
        tap_parts = {
            "tap_rows": np.concatenate([rows_hi, rows_lo, rows_hi], axis=1),
            "tap_hi": cols_hi,
            "tap_lo": cols_lo,
        }
        self.where = {}
        self.packed = self.pack(parts)
        self.tap_packed = self.pack(tap_parts)

    def pack(self, parts):
        packed, at = [], 0
        wide = max(part.shape[1] for part in parts.values())
        for name, part in parts.items():
            part = np.asarray(part, np.float32).astype(BF)
            self.where[name] = (at, part.shape[0], part.shape[1])
            fill = up_to(part.shape[0], CHUNK) - part.shape[0]
            packed.append(np.pad(part, ((0, fill), (0, wide - part.shape[1]))))
            at += part.shape[0] + fill
        return np.concatenate(packed, axis=0)

    def table(self, ref, name, block=None):
        at, rows, cols = self.where[name]
        if block is not None:
            at, rows = at + block * COL_LEN, COL_LEN
        return ref[at : at + rows, :cols]


@functools.lru_cache(maxsize=None)
def plan_of(strip_rows, width, taps):
    return Plan(strip_rows, width, taps)


def split_table(table):
    high = np.asarray(table, np.float32).astype(BF)
    low = (np.asarray(table, np.float64) - high.astype(np.float64)).astype(np.float32).astype(BF)
    return high, low


def dot(left, right):
    return lax.dot_general(left, right, (((1,), (0,)), ((), ())), preferred_element_type=F32)


def split(value):
    high = value.astype(BF)
    return high, (value - high.astype(F32)).astype(BF)


def fetch_body(
    logits_hbm,
    first_hbm,
    second_hbm,
    target_hbm,
    counts_hbm,
    taps_hbm,
    tables_hbm,
    socs_hbm,
    mask_ref,
    state_ref,
    target_ref,
    counts_ref,
    flags_ref,
    taps_ref,
    tables_ref,
    roots_ref,
    counts_smem,
    socs_smem,
    sems,
):
    pairs = (
        (logits_hbm, state_ref.at[0]),
        (counts_hbm, counts_smem),
        (target_hbm, target_ref),
        (first_hbm, state_ref.at[1]),
        (second_hbm, state_ref.at[2]),
        (taps_hbm, taps_ref),
        (tables_hbm, tables_ref),
        (socs_hbm, socs_smem),
    )
    copies = [pltpu.make_async_copy(a, b, sems.at[i]) for i, (a, b) in enumerate(pairs)]
    for copy in copies:
        copy.start()
    place, corner = lax.axis_index("tile"), lax.axis_index("corner")
    facts = (corner == 0, place == 0, place == lax.axis_size("tile") - 1)
    for i, fact in enumerate(facts):
        flags_ref[i] = jnp.full(flags_ref.shape[1:], jnp.where(fact, 1.0, 0.0), F32)
    copies[0].wait()
    mask = (1.0 / (1.0 + jnp.exp(-state_ref[0]))).astype(BF)
    mask_ref[...] = (mask.astype(F32) - MIDDLE).astype(BF)
    for copy in copies[1:]:
        copy.wait()
    for k in range(roots_ref.shape[0]):
        roots_ref[k] = jnp.sqrt(jnp.full(roots_ref.shape[1:], socs_smem[0, k], F32))
    tiles = counts_smem.shape[1]
    wide = counts_ref.shape[1] // tiles
    for tile in range(tiles):
        value = counts_smem[0, tile].astype(F32)
        counts_ref[:, tile * wide : (tile + 1) * wide] = jnp.full((8, wide), value, F32)


def fetch(
    flag_rows, mask_logits, adam_first, adam_second, target, tile_counts, taps, tables, socs_weight
):
    args = (
        mask_logits, adam_first, adam_second, target, tile_counts, taps, tables, socs_weight
    )
    shape = mask_logits.shape
    outs = (
        jax.ShapeDtypeStruct(shape, BF),
        jax.ShapeDtypeStruct((3,) + shape, F32),
        jax.ShapeDtypeStruct(target.shape, BF),
        jax.ShapeDtypeStruct((8, target.shape[1]), F32),
        jax.ShapeDtypeStruct((3, flag_rows, target.shape[1]), F32),
        jax.ShapeDtypeStruct(taps.shape, F32),
        jax.ShapeDtypeStruct(tables.shape, BF),
        jax.ShapeDtypeStruct((socs_weight.shape[1], 8, COL_LEN), F32),
    )
    return pl.pallas_call(
        fetch_body,
        out_shape=outs,
        in_specs=[pl.BlockSpec(memory_space=pltpu.HBM)] * len(args),
        out_specs=tuple(pl.BlockSpec(memory_space=pltpu.VMEM) for _ in outs),
        scratch_shapes=[
            pltpu.SMEM(tile_counts.shape, jnp.int32),
            pltpu.SMEM(socs_weight.shape, F32),
            pltpu.SemaphoreType.DMA((len(args),)),
        ],
        compiler_params=pltpu.CompilerParams(vmem_limit_bytes=4 * 1024 * 1024),
        name="fetch",
    )(*(pltpu.with_memory_space_constraint(value, pltpu.HBM) for value in args))


def spectra_body(plan, root_ref, kern_ref, table_ref, out_ref, level_ref):
    count = out_ref.shape[0]
    pad = plan.taps_pad - plan.taps
    stack, sums = [], []
    for k in range(count):
        taps = kern_ref[k // 2, :, k % 2, :]
        sums.append(jnp.sum(taps, axis=0, keepdims=True))
        stack.append(jnp.concatenate([taps, jnp.zeros((pad, plan.taps), F32)], axis=0))
    hi, lo = split(jnp.concatenate(stack, axis=0))
    sums = MIDDLE * jnp.sum(jnp.concatenate(sums, axis=0), axis=1, keepdims=True)
    sums = jnp.broadcast_to(sums, (count, COL_LEN))
    cols_hi, cols_lo = plan.table(table_ref, "tap_hi"), plan.table(table_ref, "tap_lo")
    half = dot(hi, cols_hi) + dot(lo, cols_hi) + dot(hi, cols_lo)
    for k in range(0, count, 2):
        both = []
        for part in (k, k + 1):
            one = half[part * plan.taps_pad : (part + 1) * plan.taps_pad]
            both.append(jnp.concatenate([one[:, :HALF_SPEC], one[:, HALF_SPEC:]], axis=0))
        hi, lo = split(jnp.concatenate(both, axis=1))
        spec = dot(plan.table(table_ref, "tap_rows"), jnp.concatenate([hi, hi, lo], axis=0))
        root_wide = root_ref[k // 2]
        root = root_wide[:1, :HALF_SPEC]
        for part in (k, k + 1):
            level_ref[part] = root_wide * sums[part : part + 1]
        out_ref[k] = spec[:, :HALF_SPEC] * root
        out_ref[k + 1] = spec[:, HALF_SPEC:] * root


def kernel_spectra(plan, taps, tables, roots):
    count = 2 * taps.shape[0]
    vmem = pl.BlockSpec(memory_space=pltpu.VMEM)
    return pl.pallas_call(
        functools.partial(spectra_body, plan),
        out_shape=(
            jax.ShapeDtypeStruct((count, 2 * plan.row_len, HALF_SPEC), F32),
            jax.ShapeDtypeStruct((count, 8, COL_LEN), F32),
        ),
        in_specs=[vmem] * 3,
        out_specs=(vmem, vmem),
        compiler_params=pltpu.CompilerParams(vmem_limit_bytes=4 * 1024 * 1024),
        name="spectra",
    )(roots, taps, tables)


def gradient_body(
    plan,
    dose_ref,
    mask_ref,
    target_ref,
    weight_ref,
    spec_ref,
    level_ref,
    table_ref,
    out_ref,
    s_ref,
    field_ref,
    light_ref,
    acc_ref,
    hold_ref,
    back_ref,
):
    tiles = plan.col_tiles
    rows = plan.row_len
    fr = plan.field_pad
    g = HALF_SPEC
    count = spec_ref.shape[0]

    along = []
    edges = plan.table(table_ref, "edges").astype(F32)
    for t in range(tiles):
        window = mask_ref[:, plan.starts[t] : plan.starts[t] + COL_LEN]
        a = dot(window, plan.table(table_ref, "col_fwd", t))
        if t == 0:
            a = a + (edges[0:1] + edges[1:2])
        if t == tiles - 1:
            a = a + (edges[2:3] + edges[3:4])
        along.append(jnp.concatenate([a[:, :g], a[:, g:]], axis=0).astype(BF))
    s_ref[...] = dot(plan.table(table_ref, "row_fwd"), jnp.concatenate(along, axis=1))
    light_ref[...] = jnp.zeros_like(light_ref)
    acc_ref[...] = jnp.zeros_like(acc_ref)
    chunks = [(at, at + CHUNK, at + 2 * CHUNK) for at in range(0, 2 * rows, 2 * CHUNK)]

    groups = count // GROUP

    def multiply(group):
        passed = []
        for t in range(tiles):
            lane = slice(t * g, t * g + g)
            prods = [[] for _ in range(GROUP)]
            for a, b, c in chunks:
                s_re, s_im = s_ref[a:b, lane].astype(BF), s_ref[b:c, lane].astype(BF)
                for part in range(GROUP):
                    k = GROUP * group + part
                    k_re, k_im = spec_ref[k, a:b].astype(BF), spec_ref[k, b:c].astype(BF)
                    prods[part].append(s_re * k_re - s_im * k_im)
                    prods[part].append(s_re * k_im + s_im * k_re)
            block = jnp.concatenate([jnp.concatenate(p, axis=0) for p in prods], axis=1)
            passed.append(dot(plan.table(table_ref, "row_inv"), block))
        stack = []
        for t in range(tiles):
            for part in range(GROUP):
                lane = slice(part * g, part * g + g)
                stack.append(jnp.concatenate([passed[t][:fr, lane], passed[t][fr:, lane]], axis=1))
        hold_ref[group % 2] = jnp.concatenate(stack, axis=0).astype(BF)

    def image(group):
        field = dot(hold_ref[group % 2], plan.table(table_ref, "col_inv"))
        for t in range(tiles):
            total = light_ref[t]
            for part in range(GROUP):
                at = (GROUP * t + part) * fr
                one = field[at : at + fr] + level_ref[GROUP * group + part, :1]
                field_ref[group, at : at + fr] = one
                total = total + one * one
            light_ref[t] = total

    def forward(group, carry):
        image(group)
        multiply(group + 1)
        return carry

    multiply(0)
    lax.fori_loop(0, groups - 1, forward, 0, unroll=True)
    image(groups - 1)

    dose = dose_ref[:1, :1]
    row = lax.broadcasted_iota(jnp.int32, (fr, COL_LEN), 0)
    col = lax.broadcasted_iota(jnp.int32, (fr, COL_LEN), 1)
    reach, strip = plan.reach, plan.strip_rows
    for t in range(tiles):
        lane = slice(plan.starts[t], plan.starts[t] + COL_LEN)
        resist = 1.0 / (1.0 + jnp.exp(-steep * (dose * light_ref[t] - thresh)))
        missed = resist - target_ref[:, lane].astype(F32)
        above, here, below = (weight_ref[i : i + 1, lane] for i in range(3))
        weight = jnp.where(row < reach, above, jnp.where(row < reach + strip, here, below))
        low, high = plan.bounds[t] - plan.starts[t], plan.bounds[t + 1] - plan.starts[t]
        kept = (row < plan.field_rows) & (col >= low) & (col < high)
        weight = jnp.where(kept, weight, 0.0)
        factor = 4.0 * loss_scale * steep * dose
        light_ref[t] = factor * weight * missed * resist * (1.0 - resist)

    def image_back(group, chosen):
        stack = []
        for t in chosen:
            for part in range(GROUP):
                at = (GROUP * t + part) * fr
                stack.append(light_ref[t] * field_ref[group, at : at + fr])
        inner = dot(jnp.concatenate(stack, axis=0).astype(BF), plan.table(table_ref, "col_inv_adj"))
        for i, t in enumerate(chosen):
            block = []
            for part in range(GROUP):
                at = (GROUP * i + part) * fr
                d = inner[at : at + fr]
                block.append(jnp.concatenate([d[:, :g], d[:, g:]], axis=0))
            back_ref[group % 4, t] = jnp.concatenate(block, axis=1).astype(BF)

    def multiply_back(group, chosen):
        for t in chosen:
            lane = slice(t * g, t * g + g)
            d_prod = dot(plan.table(table_ref, "row_inv_adj"), back_ref[group % 4, t])
            for a, b, c in chunks:
                sum_re, sum_im = acc_ref[a:b, lane], acc_ref[b:c, lane]
                for part in range(GROUP):
                    k = GROUP * group + part
                    k_re, k_im = spec_ref[k, a:b], spec_ref[k, b:c]
                    at = slice(part * g, part * g + g)
                    d_re, d_im = d_prod[a:b, at], d_prod[b:c, at]
                    sum_re = sum_re + (d_re * k_re + d_im * k_im)
                    sum_im = sum_im + (d_im * k_re - d_re * k_im)
                acc_ref[a:b, lane] = sum_re
                acc_ref[b:c, lane] = sum_im

    for group in range(1):
        image_back(group, range(tiles))
    for group in range(groups):
        if group + 1 < groups:
            image_back(group + 1, range(tiles))
        multiply_back(group, range(tiles))

    d_along = dot(plan.table(table_ref, "row_adj"), acc_ref[...].astype(BF))
    parts = []
    for t in range(tiles):
        lane = slice(t * g, t * g + g)
        both = jnp.concatenate([d_along[:strip, lane], d_along[strip:, lane]], axis=1).astype(BF)
        parts.append(dot(both, plan.table(table_ref, "col_adj", t)))
    blocks = []
    for b in range(plan.width // LANES):
        terms = []
        for t in range(tiles):
            at = b * LANES - plan.starts[t]
            if 0 <= at < COL_LEN:
                terms.append(parts[t][:, at : at + LANES])
        blocks.append(functools.reduce(lambda x, y: x + y, terms))
    out_ref[...] = jnp.concatenate(blocks, axis=1)


def strip_gradient(plan, mask_ext, target_ext, weights, spec, dose, tables):
    vmem = pl.BlockSpec(memory_space=pltpu.VMEM)
    count = spec[0].shape[0]
    spectrum = (2 * plan.row_len, plan.col_tiles * HALF_SPEC)
    image = (plan.col_tiles, plan.field_pad, COL_LEN)
    return pl.pallas_call(
        functools.partial(gradient_body, plan),
        out_shape=jax.ShapeDtypeStruct((plan.strip_rows, plan.width), F32),
        in_specs=[vmem] * 7,
        out_specs=vmem,
        scratch_shapes=[
            pltpu.VMEM(spectrum, F32),
            pltpu.VMEM((count // GROUP, GROUP * plan.col_tiles * plan.field_pad, COL_LEN), F32),
            pltpu.VMEM(image, F32),
            pltpu.VMEM(spectrum, F32),
            pltpu.VMEM((2, GROUP * plan.col_tiles * plan.field_pad, COL_LEN), BF),
            pltpu.VMEM((4, plan.col_tiles, 2 * plan.field_pad, GROUP * HALF_SPEC), BF),
        ],
        compiler_params=pltpu.CompilerParams(vmem_limit_bytes=12 * 1024 * 1024),
        name="gradient",
    )(dose, mask_ext, target_ext, weights, *spec, tables)


def other_corner(value):
    return lax.ppermute(value, "corner", [(0, 1), (1, 0)])


def neighbours(flags, top, bottom, blank):
    strips = lax.axis_size("tile")
    first_corner, highest, lowest = flags[:, : top.shape[0], : top.shape[1]]
    cycle = [(2 * i, 2 * i + 2) for i in range(strips - 1)] + [(2 * strips - 2, 2 * strips - 1)]
    cycle += [(2 * i + 1, 2 * i - 1) for i in range(1, strips)] + [(1, 0)]
    message = jnp.where(first_corner, bottom, top)
    got = lax.ppermute(message, ("tile", "corner"), cycle)
    shared = other_corner(got)
    above = jnp.where(highest, blank, jnp.where(first_corner, got, shared))
    below = jnp.where(lowest, blank, jnp.where(first_corner, shared, got))
    return above, below


def per_device(
    mask_logits, target, adam_first, adam_second, tile_counts, kernels, socs_weight, corner_dose
):
    strip_rows, half_width = mask_logits.shape
    width = target.shape[1]
    plan = plan_of(strip_rows, width, kernels.shape[-1])
    reach = plan.reach
    halo = 2 * reach

    def whole(own, other):
        first_corner = flags[0, : own.shape[-2], : own.shape[-1]]
        left = jnp.where(first_corner, own, other)
        right = jnp.where(first_corner, other, own)
        return jnp.concatenate([left, right], axis=-1)

    def own_half(value):
        first_corner = flags[0, : value.shape[-2], :half_width]
        return jnp.where(first_corner, value[..., :half_width], value[..., half_width:])

    def extended(above_rows, own, below_rows, total):
        have = above_rows.shape[0] + own.shape[0] + below_rows.shape[0]
        blank = jnp.zeros((total - have, own.shape[1]), own.dtype)
        return jnp.concatenate([above_rows, own, below_rows, blank], axis=0)

    tables = jnp.asarray(plan.packed)

    mask_half, state, target, counts, facts, taps, tap_tables, roots = fetch(
        up_to(max(strip_rows, halo + reach + 1), 8),
        mask_logits,
        adam_first,
        adam_second,
        target,
        tile_counts,
        kernels[0].transpose(0, 2, 1, 3),
        jnp.asarray(plan.tap_packed),
        socs_weight,
    )
    flags = facts > 0.5
    dose = jnp.broadcast_to(corner_dose[None], (8, LANES))
    counts = counts[:1]
    counts_bf = counts.astype(BF)
    other_half = other_corner(mask_half)
    mask_bf = whole(mask_half, other_half)
    above, below = neighbours(
        flags,
        jnp.concatenate([mask_bf[:halo], target[:reach], counts_bf], axis=0),
        jnp.concatenate([mask_bf[-halo:], target[-reach:], counts_bf], axis=0),
        jnp.where(jnp.arange(halo + reach + 1)[:, None] < halo, -MIDDLE, 0.0).astype(BF),
    )
    spec = kernel_spectra(plan, taps, tap_tables, roots)
    target_ext = extended(
        above[halo : halo + reach], target, below[halo : halo + reach], plan.field_pad
    )
    near = jnp.concatenate(
        [above[halo + reach :].astype(F32), counts, below[halo + reach :].astype(F32)]
    )
    near = jnp.pad(near, ((0, 5), (0, 0)))
    weights = near / (near + 4.0)
    above, below = above[:halo], below[:halo]
    mask_ext = extended(above, mask_bf, below, plan.row_len)
    state = whole(state, other_corner(state))
    partial = strip_gradient(plan, mask_ext, target_ext, weights, spec, dose, tables)

    logits, first, second = state[0], state[1], state[2]
    opacity = jax.nn.sigmoid(logits)
    for iteration in range(ITERS):
        if iteration:
            opacity = jax.nn.sigmoid(logits)
            mask_bf = (lax.reduce_precision(opacity, 8, 7) - MIDDLE).astype(BF)
            blank = jnp.full((halo, 1), -MIDDLE, BF)
            above, below = neighbours(flags, mask_bf[:halo], mask_bf[-halo:], blank)
            mask_ext = extended(above, mask_bf, below, plan.row_len)
            partial = strip_gradient(plan, mask_ext, target_ext, weights, spec, dose, tables)
        if iteration < ITERS - 1:
            summed = partial + other_corner(partial.astype(BF)).astype(F32)
        else:
            mine = own_half(partial)
            theirs = jnp.where(flags[0, :strip_rows, :half_width], partial[:, half_width:], partial[:, :half_width])
            summed = mine + other_corner(theirs.astype(BF)).astype(F32)
            opacity, logits = own_half(opacity), own_half(logits)
            first, second = own_half(first), own_half(second)
        gradient = summed * opacity * (1.0 - opacity)
        count_now = prior_steps + iteration + 1.0
        first = beta_one * first + (1.0 - beta_one) * gradient
        second = beta_two * second + (1.0 - beta_two) * gradient * gradient
        first_hat = first / (1.0 - beta_one**count_now)
        second_hat = second / (1.0 - beta_two**count_now)
        logits = logits - step_size * first_hat / (jnp.sqrt(second_hat) + adam_eps)
    return (logits, first, second)


def solution(mesh):
    return jax.shard_map(
        per_device,
        mesh=mesh,
        in_specs=(
            P(("grp", "tile"), "corner"),
            P(("grp", "tile"), None),
            P(("grp", "tile"), "corner"),
            P(("grp", "tile"), "corner"),
            P(("grp", "tile"), None),
            P("corner", None, None, None, None),
            P("corner", None),
            P("corner"),
        ),
        out_specs=(
            P(("grp", "tile"), "corner"),
            P(("grp", "tile"), "corner"),
            P(("grp", "tile"), "corner"),
        ),
        check_vma=False,
    )
```

```python
import functools
import math

import jax
import jax.numpy as jnp
import numpy as np
from jax import lax
from jax.experimental import pallas as pl
from jax.experimental.pallas import tpu as pltpu
from jax.sharding import PartitionSpec as P


ITERS = 2

steep = 8.0
thresh = 0.5
loss_scale = 20.0
step_size = 0.05
beta_one = 0.9
beta_two = 0.999
adam_eps = 1e-08
prior_steps = 1000.0

LANES = 128
HALF_SPEC = 128
MIDDLE = 0.5
COL_LEN = 2 * HALF_SPEC
CHUNK = 16
GROUP = 4

BF = jnp.bfloat16
F32 = jnp.float32


def up_to(value, unit):
    return -(-value // unit) * unit


class Plan:
    def __init__(self, strip_rows, width, taps):
        reach = taps // 2
        self.strip_rows, self.width, self.taps, self.reach = strip_rows, width, taps, reach
        self.field_rows = strip_rows + 2 * reach
        self.field_pad = up_to(self.field_rows, 8)
        self.ext_rows = strip_rows + 4 * reach
        self.row_len = up_to(self.ext_rows, 128)
        self.taps_pad = up_to(taps, 8)
        self.col_tiles = width // LANES - 1
        self.starts = [LANES * t for t in range(self.col_tiles)]
        assert width % LANES == 0 and self.col_tiles >= 2
        assert LANES > 4 * reach
        edge = LANES // 2 - 8
        self.bounds = [0] + [s + edge for s in self.starts[1:]] + [width]

        omega = 2.0 * math.pi * (np.arange(HALF_SPEC) + 0.5) / COL_LEN
        phi = 2.0 * math.pi * np.arange(self.row_len) / self.row_len
        rows = np.arange(self.row_len)

        fwd = []
        for t, start in enumerate(self.starts):
            x = start + np.arange(COL_LEN)
            keep = np.ones(COL_LEN)
            if t == 0:
                keep = keep * (x < COL_LEN - reach)
            if t == self.col_tiles - 1:
                keep = keep * (x >= start + reach)
            angle = (x - start)[:, None] * omega[None, :]
            fwd.append(np.concatenate([np.cos(angle), -np.sin(angle)], 1) * keep[:, None])
        self.col_fwd = np.stack(fwd)
        edges = []
        for x in (np.arange(-reach, 0), COL_LEN + np.arange(reach)):
            angle = x[:, None] * omega[None, :]
            edge = -MIDDLE * np.concatenate([np.cos(angle), -np.sin(angle)], 1).sum(0)
            edges += split_table(edge)
        self.edges = np.stack(edges)
        self.col_adj = self.col_fwd.transpose(0, 2, 1)

        scale = 2.0 / (COL_LEN * self.row_len)
        angle = omega[:, None] * np.arange(COL_LEN)[None, :]
        self.col_inv = np.concatenate([np.cos(angle), -np.sin(angle)], 0) * scale
        self.col_inv_adj = self.col_inv.T

        angle = phi[:, None] * rows[None, :]
        live = (rows < self.ext_rows)[None, :]
        c, s = np.cos(angle) * live, np.sin(angle) * live
        mixed = np.arange(2 * self.row_len).reshape(2, -1, CHUNK).transpose(1, 0, 2).reshape(-1)
        self.row_fwd = np.block([[c, s], [-s, c]])[mixed]
        own = slice(2 * reach, 2 * reach + strip_rows)
        self.row_adj = np.block([[c[:, own].T, -s[:, own].T], [s[:, own].T, c[:, own].T]])[:, mixed]

        angle = (np.arange(self.field_pad) + reach)[:, None] * phi[None, :]
        live = (np.arange(self.field_pad) < self.field_rows)[:, None]
        c, s = np.cos(angle) * live, np.sin(angle) * live
        self.row_inv = np.block([[c, -s], [s, c]])[:, mixed]
        self.row_inv_adj = self.row_inv.T

        tap = np.arange(taps) - reach
        angle = tap[:, None] * omega[None, :]
        self.tap_cols = np.concatenate([np.cos(angle), -np.sin(angle)], 1)
        angle = phi[:, None] * tap[None, :]
        fill = ((0, 0), (0, self.taps_pad - taps))
        c, s = np.pad(np.cos(angle), fill), np.pad(np.sin(angle), fill)
        self.tap_rows = np.block([[c, s], [-s, c]])[mixed]


        rows_hi, rows_lo = split_table(self.tap_rows)
        cols_hi, cols_lo = split_table(self.tap_cols)
        parts = {
            "col_fwd": self.col_fwd.reshape(-1, COL_LEN),
            "col_adj": self.col_adj.reshape(-1, COL_LEN),
            "col_inv": self.col_inv,
            "col_inv_adj": self.col_inv_adj,
            "row_fwd": self.row_fwd,
            "row_adj": self.row_adj,
            "row_inv": self.row_inv,
            "row_inv_adj": self.row_inv_adj,
            "edges": self.edges,
        }
        tap_parts = {
            "tap_rows": np.concatenate([rows_hi, rows_lo, rows_hi], axis=1),
            "tap_hi": cols_hi,
            "tap_lo": cols_lo,
        }
        self.where = {}
        self.packed = self.pack(parts)
        self.tap_packed = self.pack(tap_parts)

    def pack(self, parts):
        packed, at = [], 0
        wide = max(part.shape[1] for part in parts.values())
        for name, part in parts.items():
            part = np.asarray(part, np.float32).astype(BF)
            self.where[name] = (at, part.shape[0], part.shape[1])
            fill = up_to(part.shape[0], CHUNK) - part.shape[0]
            packed.append(np.pad(part, ((0, fill), (0, wide - part.shape[1]))))
            at += part.shape[0] + fill
        return np.concatenate(packed, axis=0)

    def table(self, ref, name, block=None):
        at, rows, cols = self.where[name]
        if block is not None:
            at, rows = at + block * COL_LEN, COL_LEN
        return ref[at : at + rows, :cols]


@functools.lru_cache(maxsize=None)
def plan_of(strip_rows, width, taps):
    return Plan(strip_rows, width, taps)


def split_table(table):
    high = np.asarray(table, np.float32).astype(BF)
    low = (np.asarray(table, np.float64) - high.astype(np.float64)).astype(np.float32).astype(BF)
    return high, low


def dot(left, right):
    return lax.dot_general(left, right, (((1,), (0,)), ((), ())), preferred_element_type=F32)


def split(value):
    high = value.astype(BF)
    return high, (value - high.astype(F32)).astype(BF)


def fetch_body(
    logits_hbm,
    first_hbm,
    second_hbm,
    target_hbm,
    counts_hbm,
    socs_hbm,
    mask_ref,
    state_ref,
    target_ref,
    counts_ref,
    flags_ref,
    roots_ref,
    counts_smem,
    socs_smem,
    sems,
):
    pairs = (
        (logits_hbm, state_ref.at[0]),
        (counts_hbm, counts_smem),
        (target_hbm, target_ref),
        (first_hbm, state_ref.at[1]),
        (second_hbm, state_ref.at[2]),
        (socs_hbm, socs_smem),
    )
    copies = [pltpu.make_async_copy(a, b, sems.at[i]) for i, (a, b) in enumerate(pairs)]
    for copy in copies:
        copy.start()
    place, corner = lax.axis_index("tile"), lax.axis_index("corner")
    facts = (corner == 0, place == 0, place == lax.axis_size("tile") - 1)
    for i, fact in enumerate(facts):
        flags_ref[i] = jnp.full(flags_ref.shape[1:], jnp.where(fact, 1.0, 0.0), F32)
    copies[0].wait()
    mask = (1.0 / (1.0 + jnp.exp(-state_ref[0]))).astype(BF)
    mask_ref[...] = (mask.astype(F32) - MIDDLE).astype(BF)
    for copy in copies[1:]:
        copy.wait()
    for k in range(roots_ref.shape[0]):
        roots_ref[k] = jnp.sqrt(jnp.full(roots_ref.shape[1:], socs_smem[0, k], F32))
    tiles = counts_smem.shape[1]
    wide = counts_ref.shape[1] // tiles
    for tile in range(tiles):
        value = counts_smem[0, tile].astype(F32)
        counts_ref[:, tile * wide : (tile + 1) * wide] = jnp.full((8, wide), value, F32)


def fetch(flag_rows, mask_logits, adam_first, adam_second, target, tile_counts, socs_weight):
    args = (mask_logits, adam_first, adam_second, target, tile_counts, socs_weight)
    shape = mask_logits.shape
    outs = (
        jax.ShapeDtypeStruct(shape, BF),
        jax.ShapeDtypeStruct((3,) + shape, F32),
        jax.ShapeDtypeStruct(target.shape, BF),
        jax.ShapeDtypeStruct((8, target.shape[1]), F32),
        jax.ShapeDtypeStruct((3, flag_rows, target.shape[1]), F32),
        jax.ShapeDtypeStruct((socs_weight.shape[1], 8, COL_LEN), F32),
    )
    return pl.pallas_call(
        fetch_body,
        out_shape=outs,
        in_specs=[pl.BlockSpec(memory_space=pltpu.HBM)] * len(args),
        out_specs=tuple(pl.BlockSpec(memory_space=pltpu.VMEM) for _ in outs),
        scratch_shapes=[
            pltpu.SMEM(tile_counts.shape, jnp.int32),
            pltpu.SMEM(socs_weight.shape, F32),
            pltpu.SemaphoreType.DMA((len(args),)),
        ],
        compiler_params=pltpu.CompilerParams(vmem_limit_bytes=4 * 1024 * 1024),
        name="fetch",
    )(*(pltpu.with_memory_space_constraint(value, pltpu.HBM) for value in args))


def spectra_body(
    plan, root_ref, kern_hbm, table_hbm, out_ref, level_ref, kern_ref, table_ref, sems
):
    copies = [
        pltpu.make_async_copy(kern_hbm, kern_ref, sems.at[0]),
        pltpu.make_async_copy(table_hbm, table_ref, sems.at[1]),
    ]
    for copy in copies:
        copy.start()
    for copy in copies:
        copy.wait()
    count = out_ref.shape[0]
    pad = plan.taps_pad - plan.taps
    stack, sums = [], []
    for k in range(count):
        taps = kern_ref[k // 2, :, k % 2, :]
        sums.append(jnp.sum(taps, axis=0, keepdims=True))
        stack.append(jnp.concatenate([taps, jnp.zeros((pad, plan.taps), F32)], axis=0))
    hi, lo = split(jnp.concatenate(stack, axis=0))
    sums = MIDDLE * jnp.sum(jnp.concatenate(sums, axis=0), axis=1, keepdims=True)
    sums = jnp.broadcast_to(sums, (count, COL_LEN))
    cols_hi, cols_lo = plan.table(table_ref, "tap_hi"), plan.table(table_ref, "tap_lo")
    half = dot(hi, cols_hi) + dot(lo, cols_hi) + dot(hi, cols_lo)
    for k in range(0, count, 2):
        both = []
        for part in (k, k + 1):
            one = half[part * plan.taps_pad : (part + 1) * plan.taps_pad]
            both.append(jnp.concatenate([one[:, :HALF_SPEC], one[:, HALF_SPEC:]], axis=0))
        hi, lo = split(jnp.concatenate(both, axis=1))
        spec = dot(plan.table(table_ref, "tap_rows"), jnp.concatenate([hi, hi, lo], axis=0))
        root_wide = root_ref[k // 2]
        root = root_wide[:1, :HALF_SPEC]
        for part in (k, k + 1):
            level_ref[part] = root_wide * sums[part : part + 1]
        out_ref[k] = spec[:, :HALF_SPEC] * root
        out_ref[k + 1] = spec[:, HALF_SPEC:] * root


def kernel_spectra(plan, kernels, roots):
    taps, tables = kernels[0].transpose(0, 2, 1, 3), jnp.asarray(plan.tap_packed)
    count = 2 * taps.shape[0]
    vmem = pl.BlockSpec(memory_space=pltpu.VMEM)
    return pl.pallas_call(
        functools.partial(spectra_body, plan),
        out_shape=(
            jax.ShapeDtypeStruct((count, 2 * plan.row_len, HALF_SPEC), F32),
            jax.ShapeDtypeStruct((count, 8, COL_LEN), F32),
        ),
        in_specs=[vmem] + [pl.BlockSpec(memory_space=pltpu.HBM)] * 2,
        out_specs=(vmem, vmem),
        scratch_shapes=[
            pltpu.VMEM(taps.shape, F32),
            pltpu.VMEM(tables.shape, BF),
            pltpu.SemaphoreType.DMA((2,)),
        ],
        compiler_params=pltpu.CompilerParams(vmem_limit_bytes=4 * 1024 * 1024),
        name="spectra",
    )(roots, *(pltpu.with_memory_space_constraint(value, pltpu.HBM) for value in (taps, tables)))


def gradient_body(
    plan,
    dose_ref,
    mask_ref,
    target_ref,
    weight_ref,
    spec_ref,
    level_ref,
    table_ref,
    out_ref,
    s_ref,
    field_ref,
    light_ref,
    acc_ref,
    hold_ref,
    back_ref,
):
    tiles = plan.col_tiles
    rows = plan.row_len
    fr = plan.field_pad
    g = HALF_SPEC
    count = spec_ref.shape[0]

    along = []
    edges = plan.table(table_ref, "edges").astype(F32)
    for t in range(tiles):
        window = mask_ref[:, plan.starts[t] : plan.starts[t] + COL_LEN]
        a = dot(window, plan.table(table_ref, "col_fwd", t))
        if t == 0:
            a = a + (edges[0:1] + edges[1:2])
        if t == tiles - 1:
            a = a + (edges[2:3] + edges[3:4])
        along.append(jnp.concatenate([a[:, :g], a[:, g:]], axis=0).astype(BF))
    s_ref[...] = dot(plan.table(table_ref, "row_fwd"), jnp.concatenate(along, axis=1))
    chunks = [(at, at + CHUNK, at + 2 * CHUNK) for at in range(0, 2 * rows, 2 * CHUNK)]

    groups = count // GROUP

    def multiply(group):
        passed = []
        for t in range(tiles):
            lane = slice(t * g, t * g + g)
            prods = [[] for _ in range(GROUP)]
            for a, b, c in chunks:
                s_re, s_im = s_ref[a:b, lane].astype(BF), s_ref[b:c, lane].astype(BF)
                for part in range(GROUP):
                    k = GROUP * group + part
                    k_re, k_im = spec_ref[k, a:b].astype(BF), spec_ref[k, b:c].astype(BF)
                    prods[part].append(s_re * k_re - s_im * k_im)
                    prods[part].append(s_re * k_im + s_im * k_re)
            block = jnp.concatenate([jnp.concatenate(p, axis=0) for p in prods], axis=1)
            passed.append(dot(plan.table(table_ref, "row_inv"), block))
        stack = []
        for t in range(tiles):
            for part in range(GROUP):
                lane = slice(part * g, part * g + g)
                stack.append(jnp.concatenate([passed[t][:fr, lane], passed[t][fr:, lane]], axis=1))
        hold_ref[group] = jnp.concatenate(stack, axis=0).astype(BF)

    def image(group):
        field = dot(hold_ref[group], plan.table(table_ref, "col_inv"))
        for t in range(tiles):
            total = light_ref[t] if group else 0.0
            for part in range(GROUP):
                at = (GROUP * t + part) * fr
                one = field[at : at + fr] + level_ref[GROUP * group + part, :1]
                field_ref[group, at : at + fr] = one
                total = total + one * one
            light_ref[t] = total

    multiply(0)
    for group in range(groups):
        image(group)
        if group + 1 < groups:
            multiply(group + 1)

    dose = dose_ref[:1, :1]
    row = lax.broadcasted_iota(jnp.int32, (fr, COL_LEN), 0)
    col = lax.broadcasted_iota(jnp.int32, (fr, COL_LEN), 1)
    reach, strip = plan.reach, plan.strip_rows
    for t in range(tiles):
        lane = slice(plan.starts[t], plan.starts[t] + COL_LEN)
        resist = 1.0 / (1.0 + jnp.exp(-steep * (dose * light_ref[t] - thresh)))
        missed = resist - target_ref[:, lane].astype(F32)
        above, here, below = (weight_ref[i : i + 1, lane] for i in range(3))
        weight = jnp.where(row < reach, above, jnp.where(row < reach + strip, here, below))
        low, high = plan.bounds[t] - plan.starts[t], plan.bounds[t + 1] - plan.starts[t]
        kept = (row < plan.field_rows) & (col >= low) & (col < high)
        weight = jnp.where(kept, weight, 0.0)
        factor = 4.0 * loss_scale * steep * dose
        light_ref[t] = factor * weight * missed * resist * (1.0 - resist)

    def image_back(group, chosen):
        stack = []
        for t in chosen:
            for part in range(GROUP):
                at = (GROUP * t + part) * fr
                stack.append(light_ref[t] * field_ref[group, at : at + fr])
        inner = dot(jnp.concatenate(stack, axis=0).astype(BF), plan.table(table_ref, "col_inv_adj"))
        for i, t in enumerate(chosen):
            block = []
            for part in range(GROUP):
                at = (GROUP * i + part) * fr
                d = inner[at : at + fr]
                block.append(jnp.concatenate([d[:, :g], d[:, g:]], axis=0))
            back_ref[group % 4, t] = jnp.concatenate(block, axis=1).astype(BF)

    def multiply_back(group, chosen):
        for t in chosen:
            lane = slice(t * g, t * g + g)
            d_prod = dot(plan.table(table_ref, "row_inv_adj"), back_ref[group % 4, t])
            for a, b, c in chunks:
                sum_re, sum_im = (acc_ref[a:b, lane], acc_ref[b:c, lane]) if group else (0.0, 0.0)
                for part in range(GROUP):
                    k = GROUP * group + part
                    k_re, k_im = spec_ref[k, a:b], spec_ref[k, b:c]
                    at = slice(part * g, part * g + g)
                    d_re, d_im = d_prod[a:b, at], d_prod[b:c, at]
                    sum_re = sum_re + (d_re * k_re + d_im * k_im)
                    sum_im = sum_im + (d_im * k_re - d_re * k_im)
                acc_ref[a:b, lane] = sum_re
                acc_ref[b:c, lane] = sum_im

    for t in range(tiles):
        image_back(0, (t,))
    for group in range(groups):
        for t in range(tiles):
            multiply_back(group, (t,))
            if group + 1 < groups:
                image_back(group + 1, (t,))

    d_along = dot(plan.table(table_ref, "row_adj"), acc_ref[...].astype(BF))
    parts = []
    for t in range(tiles):
        lane = slice(t * g, t * g + g)
        both = jnp.concatenate([d_along[:strip, lane], d_along[strip:, lane]], axis=1).astype(BF)
        parts.append(dot(both, plan.table(table_ref, "col_adj", t)))
    blocks = []
    for b in range(plan.width // LANES):
        terms = []
        for t in range(tiles):
            at = b * LANES - plan.starts[t]
            if 0 <= at < COL_LEN:
                terms.append(parts[t][:, at : at + LANES])
        blocks.append(functools.reduce(lambda x, y: x + y, terms))
    out_ref[...] = jnp.concatenate(blocks, axis=1)


def strip_gradient(plan, mask_ext, target_ext, weights, spec, dose, tables):
    vmem = pl.BlockSpec(memory_space=pltpu.VMEM)
    count = spec[0].shape[0]
    spectrum = (2 * plan.row_len, plan.col_tiles * HALF_SPEC)
    image = (plan.col_tiles, plan.field_pad, COL_LEN)
    return pl.pallas_call(
        functools.partial(gradient_body, plan),
        out_shape=jax.ShapeDtypeStruct((plan.strip_rows, plan.width), F32),
        in_specs=[vmem] * 7,
        out_specs=vmem,
        scratch_shapes=[
            pltpu.VMEM(spectrum, F32),
            pltpu.VMEM((count // GROUP, GROUP * plan.col_tiles * plan.field_pad, COL_LEN), F32),
            pltpu.VMEM(image, F32),
            pltpu.VMEM(spectrum, F32),
            pltpu.VMEM((count // GROUP, GROUP * plan.col_tiles * plan.field_pad, COL_LEN), BF),
            pltpu.VMEM((4, plan.col_tiles, 2 * plan.field_pad, GROUP * HALF_SPEC), BF),
        ],
        compiler_params=pltpu.CompilerParams(vmem_limit_bytes=12 * 1024 * 1024),
        name="gradient",
    )(dose, mask_ext, target_ext, weights, *spec, tables)


def other_corner(value):
    return lax.ppermute(value, "corner", [(0, 1), (1, 0)])


def neighbours(flags, top, bottom, blank):
    strips = lax.axis_size("tile")
    first_corner, highest, lowest = flags[:, : top.shape[0], : top.shape[1]]
    cycle = [(2 * i, 2 * i + 2) for i in range(strips - 1)] + [(2 * strips - 2, 2 * strips - 1)]
    cycle += [(2 * i + 1, 2 * i - 1) for i in range(1, strips)] + [(1, 0)]
    message = jnp.where(first_corner, bottom, top)
    got = lax.ppermute(message, ("tile", "corner"), cycle)
    shared = other_corner(got)
    above = jnp.where(highest, blank, jnp.where(first_corner, got, shared))
    below = jnp.where(lowest, blank, jnp.where(first_corner, shared, got))
    return above, below


def per_device(
    mask_logits, target, adam_first, adam_second, tile_counts, kernels, socs_weight, corner_dose
):
    strip_rows, half_width = mask_logits.shape
    width = target.shape[1]
    plan = plan_of(strip_rows, width, kernels.shape[-1])
    reach = plan.reach
    halo = 2 * reach

    def whole(own, other):
        first_corner = flags[0, : own.shape[-2], : own.shape[-1]]
        left = jnp.where(first_corner, own, other)
        right = jnp.where(first_corner, other, own)
        return jnp.concatenate([left, right], axis=-1)

    def own_half(value):
        first_corner = flags[0, : value.shape[-2], :half_width]
        return jnp.where(first_corner, value[..., :half_width], value[..., half_width:])

    def extended(above_rows, own, below_rows, total):
        have = above_rows.shape[0] + own.shape[0] + below_rows.shape[0]
        blank = jnp.zeros((total - have, own.shape[1]), own.dtype)
        return jnp.concatenate([above_rows, own, below_rows, blank], axis=0)

    tables = jnp.asarray(plan.packed)

    mask_half, state, target, counts, facts, roots = fetch(
        up_to(max(strip_rows, halo + reach + 1), 8),
        mask_logits,
        adam_first,
        adam_second,
        target,
        tile_counts,
        socs_weight,
    )
    flags = facts > 0.5
    dose = jnp.broadcast_to(corner_dose[None], (8, LANES))
    counts = counts[:1]
    counts_bf = counts.astype(BF)
    other_half = other_corner(mask_half)
    mask_bf = whole(mask_half, other_half)
    above, below = neighbours(
        flags,
        jnp.concatenate([mask_bf[:halo], target[:reach], counts_bf], axis=0),
        jnp.concatenate([mask_bf[-halo:], target[-reach:], counts_bf], axis=0),
        jnp.where(jnp.arange(halo + reach + 1)[:, None] < halo, -MIDDLE, 0.0).astype(BF),
    )
    spec = kernel_spectra(plan, kernels, roots)
    target_ext = extended(
        above[halo : halo + reach], target, below[halo : halo + reach], plan.field_pad
    )
    near = jnp.concatenate(
        [above[halo + reach :].astype(F32), counts, below[halo + reach :].astype(F32)]
    )
    near = jnp.pad(near, ((0, 5), (0, 0)))
    weights = near / (near + 4.0)
    above, below = above[:halo], below[:halo]
    mask_ext = extended(above, mask_bf, below, plan.row_len)
    state = whole(state, other_corner(state))
    partial = strip_gradient(plan, mask_ext, target_ext, weights, spec, dose, tables)

    logits, first, second = state[0], state[1], state[2]
    opacity = jax.nn.sigmoid(logits)
    for iteration in range(ITERS):
        if iteration:
            opacity = jax.nn.sigmoid(logits)
            mask_bf = (lax.reduce_precision(opacity, 8, 7) - MIDDLE).astype(BF)
            blank = jnp.full((halo, 1), -MIDDLE, BF)
            above, below = neighbours(flags, mask_bf[:halo], mask_bf[-halo:], blank)
            mask_ext = extended(above, mask_bf, below, plan.row_len)
            partial = strip_gradient(plan, mask_ext, target_ext, weights, spec, dose, tables)
        if iteration < ITERS - 1:
            summed = partial + other_corner(partial.astype(BF)).astype(F32)
        else:
            mine = own_half(partial)
            theirs = jnp.where(flags[0, :strip_rows, :half_width], partial[:, half_width:], partial[:, :half_width])
            summed = mine + other_corner(theirs.astype(BF)).astype(F32)
            opacity, logits = own_half(opacity), own_half(logits)
            first, second = own_half(first), own_half(second)
        gradient = summed * opacity * (1.0 - opacity)
        count_now = prior_steps + iteration + 1.0
        first = beta_one * first + (1.0 - beta_one) * gradient
        second = beta_two * second + (1.0 - beta_two) * gradient * gradient
        first_hat = first / (1.0 - beta_one**count_now)
        second_hat = second / (1.0 - beta_two**count_now)
        logits = logits - step_size * first_hat / (jnp.sqrt(second_hat) + adam_eps)
    return (logits, first, second)


def solution(mesh):
    return jax.shard_map(
        per_device,
        mesh=mesh,
        in_specs=(
            P(("grp", "tile"), "corner"),
            P(("grp", "tile"), None),
            P(("grp", "tile"), "corner"),
            P(("grp", "tile"), "corner"),
            P(("grp", "tile"), None),
            P("corner", None, None, None, None),
            P("corner", None),
            P("corner"),
        ),
        out_specs=(
            P(("grp", "tile"), "corner"),
            P(("grp", "tile"), "corner"),
            P(("grp", "tile"), "corner"),
        ),
        check_vma=False,
    )
```
